256 devices in a mesh: dp: 4 (over y), expert: 64 (over x, z, core).
Axes of the slice: x: 4, y: 4, z: 8, core: 2. Of those that a mesh axis runs over, the one named last changes fastest.
Arguments:
- tokens: bfloat16 [64, 88, 4096], P('expert'), may hold values from -6 to 6
- routing: int32 [64, 88, 8], P('expert'), may hold values from 0 to 63, as said below
- combine: float32 [64, 88, 8], P('expert'), may hold values from 0.05 to 0.5
- w_gate: bfloat16 [64, 4096, 1536], P('expert', None, 'dp'), may hold values from -0.09375 to 0.09375
- w_up: bfloat16 [64, 4096, 1536], P('expert', None, 'dp'), may hold values from -0.09375 to 0.09375
- w_down: bfloat16 [64, 1536, 4096], P('expert', 'dp'), may hold values from -0.15625 to 0.15625
Outputs:
- mixed: bfloat16 [64, 88, 4096], P('expert', None, 'dp')
The draws below stay inside these ranges and needn't reach their ends.
Inputs may be any that keep to these rules, and one draw needn't show every extreme that they name: `routing`: each token names 8 different experts. In every group one expert, the same in all groups, is chosen by exactly 44 tokens; every other expert is chosen by 5 to 13 tokens of a group, and one of them, the same in all groups, by exactly 13 tokens of every group.
All inputs are finite; a program needn't handle non-finite values.
Results may differ from the reference program's by a relative error of at most 0.015.
Values may be sent and summed in bfloat16 or wider, within the bound.
A program may use at most 128 MiB of HBM per device.

```python
import math
import jax
import jax.numpy as jnp
from jax import lax

D = 4096
FF = 1536
TOP = 8
EXPERTS = 64
GROUP_TOK = 88
GROUPS = 64
CAP = 13
LOW = 5
HOT_CAP = 44
N_DP = 4


def group_routes(key, hot_expert, full_cold):
    cold_count = EXPERTS - 1
    spare = CAP - LOW
    extra_total = GROUP_TOK * TOP - HOT_CAP - cold_count * LOW
    first_key, second_key, third_key = jax.random.split(key, 3)
    slot_total = cold_count * spare
    scores = jax.random.permutation(first_key, slot_total).astype(jnp.int32)
    slot_owner = jnp.arange(slot_total, dtype=jnp.int32) // spare
    scores = jnp.where(slot_owner == full_cold, scores - slot_total, scores)
    order = jnp.argsort(scores)
    slot_place = jnp.zeros((slot_total,), jnp.int32).at[order].set(jnp.arange(slot_total, dtype=jnp.int32))
    taken = (slot_place < extra_total).astype(jnp.int32)
    cold_counts = LOW + jnp.sum(taken.reshape(cold_count, spare), axis=1)
    expert_ids = jnp.arange(EXPERTS, dtype=jnp.int32)
    cold_index = jnp.clip(expert_ids - (expert_ids > hot_expert).astype(jnp.int32), 0, cold_count - 1)
    counts = jnp.where(expert_ids == hot_expert, HOT_CAP, cold_counts[cold_index])
    bounds = jnp.cumsum(counts).astype(jnp.int32)
    tickets = jnp.arange(GROUP_TOK * TOP, dtype=jnp.int32)
    expert_of = jnp.sum((tickets[:, None] >= bounds[None, :]).astype(jnp.int32), axis=1)
    table = expert_of.reshape(TOP, GROUP_TOK).T
    table = table[jax.random.permutation(second_key, GROUP_TOK)]
    shuffle = jax.random.randint(third_key, (GROUP_TOK, TOP), 0, 1 << 20) * TOP + jnp.arange(TOP, dtype=jnp.int32)[None, :]
    table = jnp.take_along_axis(table, jnp.argsort(shuffle, axis=1), axis=1)
    return table.astype(jnp.int32)


def draw_routing(key, part):
    hot_expert = jax.random.randint(jax.random.fold_in(key, 11), (), 0, EXPERTS)
    full_cold = jax.random.randint(jax.random.fold_in(key, 12), (), 0, EXPERTS - 1)
    group_keys = jax.random.split(jax.random.fold_in(key, 13), GROUPS)
    return jax.vmap(lambda one_key: group_routes(one_key, hot_expert, full_cold))(group_keys)


def block_levels(own_key, shape, shards, least, high):
    factor_of, own = 1.0, jax.random.fold_in(own_key, 6)
    for dim, blocks in shards:
        steps = jnp.exp(jax.random.uniform(jax.random.fold_in(own, dim), (blocks,), jnp.float32, least / len(shards), high / len(shards)))
        factor_of = factor_of * jnp.repeat(steps, shape[dim] // blocks).reshape([-1 if axis == dim else 1 for axis in range(len(shape))])
    return factor_of


def bell_draw(key, dims, spread, bound, shards=(), kind=jnp.bfloat16):
    drawn = jax.random.normal(key, dims, jnp.float32) * spread
    if len(shards) > 0:
        drawn = block_levels(key, dims, shards, -0.22, 0.18) * drawn
    return jnp.clip(drawn, min=-bound, max=bound).astype(kind)


def setup_inputs(seed: int = 0) -> dict:
    key_list = jax.random.split(jax.random.key(seed), 7)
    tokens = bell_draw(key_list[0], (GROUPS, GROUP_TOK, D), 1.0, 6.0, ((0, 64),))
    routing = draw_routing(jax.random.fold_in(key_list[6], 71), 0)
    combine = jnp.clip(jnp.exp(math.log(0.5) - 2.3025851 * jax.random.uniform(key_list[2], (GROUPS, GROUP_TOK, TOP), jnp.float32) ** block_levels(key_list[2], (GROUPS, GROUP_TOK, TOP), ((0, 64),), -0.2, 0.2)), 0.05, 0.5)
    w_gate = bell_draw(key_list[3], (EXPERTS, D, FF), D ** -0.5, 0.09375, ((0, 64), (2, 4)))
    w_up = bell_draw(key_list[4], (EXPERTS, D, FF), D ** -0.5, 0.09375, ((0, 64), (2, 4)))
    w_down = bell_draw(key_list[5], (EXPERTS, FF, D), FF ** -0.5, 0.15625, ((0, 64), (1, 4)))
    return {"tokens": tokens, "routing": routing, "combine": combine, "w_gate": w_gate, "w_up": w_up, "w_down": w_down}


def expert_rows(inputs, gate_mat, up_mat, down_mat, quarter):
    gate_val = jnp.dot(inputs, gate_mat, preferred_element_type=jnp.float32)
    up_val = jnp.dot(inputs, up_mat, preferred_element_type=jnp.float32)
    hidden = (jax.nn.silu(gate_val) * up_val).astype(jnp.bfloat16)
    total = jnp.zeros((inputs.shape[0], down_mat.shape[1]), jnp.float32)
    for part_idx in range(N_DP):
        lower = part_idx * quarter
        piece = jnp.dot(hidden[:, lower:lower + quarter], down_mat[lower:lower + quarter], preferred_element_type=jnp.float32)
        total = total + lax.optimization_barrier(piece.astype(jnp.bfloat16)).astype(jnp.float32)
    return total.astype(jnp.bfloat16)


def reference(tokens, routing, combine, w_gate, w_up, w_down):
    model_width = tokens.shape[2]
    token_rows = tokens.reshape(-1, model_width)
    num_tokens = token_rows.shape[0]
    top_k = routing.shape[2]
    pick_ids = routing.reshape(-1).astype(jnp.int32)
    assigns = pick_ids.shape[0]
    experts = w_gate.shape[0]
    quarter = w_gate.shape[2] // N_DP
    padded = jnp.concatenate([token_rows, jnp.zeros((1, model_width), token_rows.dtype)], axis=0)
    weight_flat = jnp.concatenate([combine.reshape(-1).astype(jnp.float32), jnp.zeros((1,), jnp.float32)], axis=0)
    counts = jnp.zeros((experts,), jnp.int32).at[pick_ids].add(jnp.ones((assigns,), jnp.int32))
    hot_expert = jnp.argmax(counts).astype(jnp.int32)
    positions = jnp.arange(assigns, dtype=jnp.int32)

    def one_expert(result, expert_id, capacity):
        member = (pick_ids == expert_id).astype(jnp.int32)
        slot_rank = (jnp.cumsum(member) - 1).astype(jnp.int32)
        where_to = jnp.where(member == 1, slot_rank, capacity).astype(jnp.int32)
        sources = jnp.full((capacity,), assigns, jnp.int32).at[where_to].set(positions, mode="drop")
        owner_tok = (sources // top_k).astype(jnp.int32)
        inputs = jnp.take(padded, owner_tok, axis=0)
        outputs = expert_rows(inputs, w_gate[expert_id], w_up[expert_id], w_down[expert_id], quarter)
        scaled = jnp.take(weight_flat, sources)[:, None] * outputs.astype(jnp.float32)
        return result.at[owner_tok].add(scaled)

    result = jnp.zeros((num_tokens + 1, model_width), jnp.float32)
    result = one_expert(result, hot_expert, GROUPS * HOT_CAP)

    def cold_step(carried, index):
        expert_id = (index + (index >= hot_expert).astype(jnp.int32)).astype(jnp.int32)
        return one_expert(carried, expert_id, GROUPS * CAP), index

    result = lax.scan(cold_step, result, jnp.arange(experts - 1, dtype=jnp.int32))[0]
    return result[:num_tokens].astype(jnp.bfloat16).reshape(tokens.shape)
```

```python
import functools

import jax
import jax.numpy as jnp
import numpy as np
from jax import lax
from jax.experimental import pallas as pl
from jax.experimental.pallas import tpu as pltpu
from jax.sharding import PartitionSpec as P

CAP = 13
HOT_CAP = 44
SLOT = 16
BLOCKS = 4
MESH = pl.DeviceIdType.MESH
VMEM = pltpu.VMEM
BF16 = jnp.bfloat16
F32 = jnp.float32


def dot(a, b):
    return jnp.dot(a, b, preferred_element_type=F32)


def cold_kernel(
    tok, pick, mix_hi, mix_lo, pack, unpack, gate_hbm, up_hbm, down_hbm, out,
    sent, got, rows, part, relay_up, relay_down, from_up, from_down, spread, back,
    w_gate, w_up, w_down, acc_gate, acc_up,
    load_sem, disp_send, disp_recv, y_send, y_recv, back_send, back_recv,
):
    n_dp, experts = rows.shape[0], got.shape[0] // SLOT
    per = experts // BLOCKS
    padded, packed = per * SLOT, per * CAP
    quarter = sent.shape[1]
    half = quarter // 2
    me, mine = lax.axis_index("dp"), lax.axis_index("expert")
    my_block, my_place = mine // per, mine % per
    above, below, across = (me + 1) % n_dp, (me + n_dp - 1) % n_dp, (me + 2) % n_dp

    loads = [
        pltpu.make_async_copy(src, dst, load_sem.at[i])
        for i, (src, dst) in enumerate(((gate_hbm, w_gate), (up_hbm, w_up), (down_hbm, w_down)))
    ]
    for load in loads:
        load.start()

    own_cols = pl.ds(pl.multiple_of(me * quarter, 128), quarter)

    @pl.loop(0, BLOCKS)
    def _(b):
        at = pl.ds(pl.multiple_of(b * padded, padded), padded)
        sent[at, :] = dot(pick[at, :], tok[:, own_cols]).astype(BF16)

    def slot(i):
        return pl.ds(pl.multiple_of(i * SLOT, SLOT), SLOT)

    own = slot(mine)
    got[own, :] = sent[own, :]

    def exchange(src, dst, to, send_sem, recv_sem):
        return pltpu.make_async_remote_copy(
            src_ref=src.at[slot(to), :], dst_ref=dst.at[own, :], send_sem=send_sem, recv_sem=recv_sem,
            device_id={"expert": to}, device_id_type=MESH,
        )

    for j in range(BLOCKS):

        @pl.loop(1 if j == 0 else 0, per)
        def _(i, j=j):
            to = ((my_block + j) % BLOCKS) * per + (my_place + i) % per
            exchange(sent, got, to, disp_send, disp_recv.at[j]).start()

    def across_dp(kind, j, src, dst, to):
        return pltpu.make_async_remote_copy(
            src_ref=src, dst_ref=dst, send_sem=y_send.at[kind, j], recv_sem=y_recv.at[kind, j],
            device_id={"dp": to}, device_id_type=MESH,
        )

    def block_of(j):
        return (my_block + BLOCKS - j) % BLOCKS

    def packed_at(j):
        return pl.ds(pl.multiple_of(block_of(j) * packed, 16), packed)

    def padded_at(j):
        return pl.ds(pl.multiple_of(block_of(j) * padded, padded), padded)

    left, right = pl.ds(0, half), pl.ds(half, half)
    copies = {}

    def start(kind, j, src, dst, to):
        copies[kind, j] = across_dp(kind, j, src, dst, to)
        copies[kind, j].start()

    def gather_rows(j):
        take = per - 1 if j == 0 else per
        pltpu.make_async_copy(
            got.at[pl.ds(0, take * SLOT), :], got.at[pl.ds(0, take * SLOT), :], disp_recv.at[j]
        ).wait()
        at = packed_at(j)
        rows[me, at, :] = dot(pack[...], got[padded_at(j), :]).astype(BF16)
        start(0, j, rows.at[me, at, :], rows.at[me, at, :], above)
        start(1, j, rows.at[me, at, :], rows.at[me, at, :], below)

    def forward_rows(j):
        at = packed_at(j)
        copies[0, j].wait_recv()
        start(2, j, rows.at[below, at, left], rows.at[below, at, left], above)
        copies[1, j].wait_recv()
        start(3, j, rows.at[above, at, right], rows.at[above, at, right], below)

    def compute(j):
        at = packed_at(j)
        copies[2, j].wait_recv()
        copies[3, j].wait_recv()
        acc_gate[...] = jnp.zeros_like(acc_gate)
        acc_up[...] = jnp.zeros_like(acc_up)

        @pl.loop(0, n_dp)
        def _(q):
            depth = pl.ds(pl.multiple_of(q * quarter, quarter), quarter)
            acc_gate[...] += dot(rows[q, at, :], w_gate[depth, :])
            acc_up[...] += dot(rows[q, at, :], w_up[depth, :])

        hidden = (jax.nn.silu(acc_gate[...]) * acc_up[...]).astype(BF16)

        @pl.loop(0, n_dp)
        def _(i):
            q = (across + i) % n_dp
            cols = pl.ds(pl.multiple_of(q * quarter, quarter), quarter)
            part[q, at, :] = dot(hidden, w_down[:, cols]).astype(BF16)

        start(4, j, part.at[across, at, left], relay_up.at[at, :], above)
        start(5, j, part.at[across, at, right], relay_down.at[at, :], below)

    def relay(j):
        at = packed_at(j)
        copies[4, j].wait_recv()
        part[above, at, left] = (part[above, at, left].astype(F32) + relay_up[at, :].astype(F32)).astype(BF16)
        start(6, j, part.at[above, at, :], from_down.at[at, :], above)
        copies[5, j].wait_recv()
        part[below, at, right] = (part[below, at, right].astype(F32) + relay_down[at, :].astype(F32)).astype(BF16)
        start(7, j, part.at[below, at, :], from_up.at[at, :], below)

    def send_back(j):
        at, wide = packed_at(j), padded_at(j)
        copies[6, j].wait_recv()
        copies[7, j].wait_recv()
        total = part[me, at, :].astype(F32) + from_down[at, :].astype(F32) + from_up[at, :].astype(F32)
        spread[wide, :] = dot(unpack[...], total.astype(BF16)).astype(BF16)
        if j == 0:
            back[own, :] = spread[own, :]

        @pl.loop(1 if j == 0 else 0, per)
        def _(i):
            to = block_of(j) * per + (my_place + i) % per
            exchange(spread, back, to, back_send, back_recv).start()

    stages = (gather_rows, forward_rows, compute, relay, send_back)
    delays = (0, 1, 2, 3, 4)
    for step in range(BLOCKS + delays[-1]):
        for stage, delay in zip(stages, delays):
            j = step - delay
            if 0 <= j < BLOCKS:
                if stage is compute and j == 0:
                    for load in loads:
                        load.wait()
                stage(j)

    others = pl.ds(0, (experts - 1) * SLOT)
    pltpu.make_async_copy(back.at[others, :], back.at[others, :], back_recv).wait()
    down_rows = (((0,), (0,)), ((), ()))
    mixed = lax.dot_general(mix_hi[...], back[...], down_rows, preferred_element_type=F32)
    out[...] = mixed + lax.dot_general(mix_lo[...], back[...], down_rows, preferred_element_type=F32)

    pltpu.make_async_copy(sent.at[others, :], sent.at[others, :], disp_send).wait()
    pltpu.make_async_copy(spread.at[others, :], spread.at[others, :], back_send).wait()
    for copy in copies.values():
        copy.wait_send()


def cold_experts(tokens, pick, mix_hi, mix_lo, w_gate, w_up, w_down):
    group_tok, width = tokens.shape
    experts, n_dp = lax.axis_size("expert"), lax.axis_size("dp")
    units, quarter, per = w_gate.shape[1], width // n_dp, experts // BLOCKS
    slots, held = experts * SLOT, experts * CAP
    block = per * CAP
    place = np.arange(block)
    wanted = (place // CAP) * SLOT + place % CAP
    pack = jnp.asarray(wanted[:, None] == np.arange(per * SLOT)[None, :], BF16)
    unpack = jnp.asarray(wanted[None, :] == np.arange(per * SLOT)[:, None], BF16)
    vmem, anywhere = pl.BlockSpec(memory_space=VMEM), pl.BlockSpec(memory_space=pl.ANY)
    dma = pltpu.SemaphoreType.DMA
    return pl.pallas_call(
        cold_kernel,
        name="cold_experts",
        out_shape=jax.ShapeDtypeStruct((group_tok, quarter), F32),
        in_specs=[vmem] * 6 + [anywhere] * 3,
        out_specs=vmem,
        scratch_shapes=[
            VMEM((slots, quarter), BF16),
            VMEM((slots, quarter), BF16),
            VMEM((n_dp, held, quarter), BF16),
            VMEM((n_dp, held, quarter), BF16),
            VMEM((held, quarter // 2), BF16),
            VMEM((held, quarter // 2), BF16),
            VMEM((held, quarter), BF16),
            VMEM((held, quarter), BF16),
            VMEM((slots, quarter), BF16),
            VMEM((slots, quarter), BF16),
            VMEM((width, units), BF16),
            VMEM((width, units), BF16),
            VMEM((units, width), BF16),
            VMEM((block, units), F32),
            VMEM((block, units), F32),
            dma((3,)),
            dma,
            dma((BLOCKS,)),
            dma((8, BLOCKS)),
            dma((8, BLOCKS)),
            dma,
            dma,
        ],
        compiler_params=pltpu.CompilerParams(vmem_limit_bytes=56 << 20, has_side_effects=True),
        cost_estimate=pl.CostEstimate(
            flops=6 * held * width * units, bytes_accessed=60 << 20, transcendentals=held * units
        ),
    )(tokens, pick, mix_hi, mix_lo, pack, unpack, w_gate, w_up, w_down)


def expert_partial(inputs, gate_mat, up_mat, down_mat):
    gate_val = jnp.dot(inputs, gate_mat, preferred_element_type=F32)
    up_val = jnp.dot(inputs, up_mat, preferred_element_type=F32)
    hidden = (jax.nn.silu(gate_val) * up_val).astype(BF16)
    return jnp.dot(hidden, down_mat, preferred_element_type=F32)


def split_weight(weight):
    high = lax.reduce_precision(weight, 8, 7)
    return high.astype(BF16), (weight - high).astype(BF16)


def local(tokens, routing, combine, w_gate, w_up, w_down):
    group_rows, chosen, mixing = tokens[0], routing[0], combine[0]
    w_gate, w_up, w_down = w_gate[0], w_up[0], w_down[0]
    group_tok = chosen.shape[0]
    experts = lax.axis_size("expert")
    ids = jnp.arange(experts, dtype=jnp.int32)
    hit = chosen.T[None, :, :] == ids[:, None, None]
    member = jnp.sum(hit.astype(F32), axis=1)
    weight = jnp.sum(jnp.where(hit, mixing.T[None, :, :], 0.0), axis=1)
    earlier = jnp.asarray(np.triu(np.ones((group_tok, group_tok)), 1), BF16)
    before = jnp.dot(member.astype(BF16), earlier, preferred_element_type=F32)
    hot_expert = jnp.argmax(jnp.sum(member, axis=1)).astype(jnp.int32)
    is_hot = (ids == hot_expert)[:, None]
    rank = jnp.where(member > 0, before, -1.0)

    picked = jnp.where(is_hot, -1.0, rank)[:, None, :] == jnp.arange(SLOT, dtype=F32)[None, :, None]
    high, low = split_weight(weight)
    zero = jnp.zeros((), BF16)
    pick = picked.astype(BF16).reshape(experts * SLOT, group_tok)
    mix_hi = jnp.where(picked, high[:, None, :], zero).reshape(experts * SLOT, group_tok)
    mix_lo = jnp.where(picked, low[:, None, :], zero).reshape(experts * SLOT, group_tok)

    hot_rank = jnp.sum(jnp.where(is_hot, rank, 0.0), axis=0)
    hot_weight = jnp.sum(jnp.where(is_hot, weight, 0.0), axis=0)
    hot_pick = hot_rank[None, :] == jnp.arange(HOT_CAP, dtype=F32)[:, None]

    owned = lax.axis_index("expert") == hot_expert
    hot_gate, hot_up, hot_down = lax.psum(
        tuple(jnp.where(owned, w, jnp.zeros_like(w)) for w in (w_gate, w_up, w_down)), "expert"
    )
    cold = cold_experts(group_rows, pick, mix_hi, mix_lo, w_gate, w_up, w_down)
    hot_rows = jnp.dot(hot_pick.astype(BF16), group_rows, preferred_element_type=F32).astype(BF16)
    hot_part = expert_partial(hot_rows, hot_gate, hot_up, hot_down)
    hot_sum = lax.psum_scatter(hot_part.astype(BF16), "dp", scatter_dimension=1, tiled=True)
    hot_mix = jnp.where(hot_pick, hot_weight[None, :], 0.0)
    hot = lax.dot_general(
        hot_mix, hot_sum.astype(F32), (((0,), (0,)), ((), ())),
        precision=lax.Precision.HIGHEST, preferred_element_type=F32,
    )
    return (cold + hot).astype(BF16)[None]


def solution(mesh):
    placed = (
        P("expert", None, None),
        P("expert", None, None),
        P("expert", None, None),
        P("expert", None, "dp"),
        P("expert", None, "dp"),
        P("expert", "dp", None),
    )
    return jax.shard_map(
        local, mesh=mesh, in_specs=placed, out_specs=P("expert", None, "dp"), check_vma=False
    )
```

```python
import functools

import jax
import jax.numpy as jnp
import numpy as np
from jax import lax
from jax.experimental import pallas as pl
from jax.experimental.pallas import tpu as pltpu
from jax.sharding import PartitionSpec as P

CAP = 13
HOT_CAP = 44
SLOT = 16
BLOCKS = 4
MESH = pl.DeviceIdType.MESH
VMEM = pltpu.VMEM
BF16 = jnp.bfloat16
F32 = jnp.float32


def dot(a, b):
    return jnp.dot(a, b, preferred_element_type=F32)


def cold_kernel(
    tok, pick, mix_hi, mix_lo, pack, unpack, gate_hbm, up_hbm, down_hbm, out,
    sent, got, rows, part, relay_up, relay_down, from_up, from_down, spread, back,
    w_gate, w_up, w_down, acc_gate, acc_up,
    load_sem, disp_send, disp_recv, y_send, y_recv, back_send, back_recv,
):
    n_dp, experts = rows.shape[0], got.shape[0] // SLOT
    per = experts // BLOCKS
    padded, packed = per * SLOT, per * CAP
    quarter = sent.shape[1]
    half = quarter // 2
    me, mine = lax.axis_index("dp"), lax.axis_index("expert")
    my_block, my_place = mine // per, mine % per
    above, below, across = (me + 1) % n_dp, (me + n_dp - 1) % n_dp, (me + 2) % n_dp

    loads = [
        pltpu.make_async_copy(src, dst, load_sem.at[i])
        for i, (src, dst) in enumerate(((gate_hbm, w_gate), (up_hbm, w_up), (down_hbm, w_down)))
    ]
    for load in loads:
        load.start()

    own_cols = pl.ds(pl.multiple_of(me * quarter, 128), quarter)

    @pl.loop(0, BLOCKS)
    def _(b):
        at = pl.ds(pl.multiple_of(b * padded, padded), padded)
        sent[at, :] = dot(pick[at, :], tok[:, own_cols]).astype(BF16)

    def slot(i):
        return pl.ds(pl.multiple_of(i * SLOT, SLOT), SLOT)

    own = slot(mine)
    got[own, :] = sent[own, :]

    def exchange(src, dst, to, send_sem, recv_sem):
        return pltpu.make_async_remote_copy(
            src_ref=src.at[slot(to), :], dst_ref=dst.at[own, :], send_sem=send_sem, recv_sem=recv_sem,
            device_id={"expert": to}, device_id_type=MESH,
        )

    for j in range(BLOCKS):

        @pl.loop(1 if j == 0 else 0, per)
        def _(i, j=j):
            to = ((my_block + j) % BLOCKS) * per + (my_place + i) % per
            exchange(sent, got, to, disp_send, disp_recv.at[j]).start()

    def across_dp(kind, j, src, dst, to):
        return pltpu.make_async_remote_copy(
            src_ref=src, dst_ref=dst, send_sem=y_send.at[kind, j], recv_sem=y_recv.at[kind, j],
            device_id={"dp": to}, device_id_type=MESH,
        )

    def block_of(j):
        return (my_block + BLOCKS - j) % BLOCKS

    def packed_at(j):
        return pl.ds(pl.multiple_of(block_of(j) * packed, 16), packed)

    def padded_at(j):
        return pl.ds(pl.multiple_of(block_of(j) * padded, padded), padded)

    left, right = pl.ds(0, half), pl.ds(half, half)
    copies = {}

    def start(kind, j, src, dst, to):
        copies[kind, j] = across_dp(kind, j, src, dst, to)
        copies[kind, j].start()

    def gather_rows(j):
        take = per - 1 if j == 0 else per
        pltpu.make_async_copy(
            got.at[pl.ds(0, take * SLOT), :], got.at[pl.ds(0, take * SLOT), :], disp_recv.at[j]
        ).wait()
        at = packed_at(j)
        rows[me, at, :] = dot(pack[...], got[padded_at(j), :]).astype(BF16)
        start(0, j, rows.at[me, at, :], rows.at[me, at, :], above)
        start(1, j, rows.at[me, at, :], rows.at[me, at, :], below)

    def forward_rows(j):
        at = packed_at(j)
        copies[0, j].wait_recv()
        start(2, j, rows.at[below, at, left], rows.at[below, at, left], above)
        copies[1, j].wait_recv()
        start(3, j, rows.at[above, at, right], rows.at[above, at, right], below)

    def compute(j):
        at = packed_at(j)
        copies[2, j].wait_recv()
        copies[3, j].wait_recv()
        acc_gate[...] = jnp.zeros_like(acc_gate)
        acc_up[...] = jnp.zeros_like(acc_up)

        @pl.loop(0, n_dp)
        def _(q):
            depth = pl.ds(pl.multiple_of(q * quarter, quarter), quarter)
            acc_gate[...] += dot(rows[q, at, :], w_gate[depth, :])
            acc_up[...] += dot(rows[q, at, :], w_up[depth, :])

        hidden = (jax.nn.silu(acc_gate[...]) * acc_up[...]).astype(BF16)

        @pl.loop(0, n_dp)
        def _(i):
            q = (across + i) % n_dp
            cols = pl.ds(pl.multiple_of(q * quarter, quarter), quarter)
            part[q, at, :] = dot(hidden, w_down[:, cols]).astype(BF16)

        start(4, j, part.at[across, at, left], relay_up.at[at, :], above)
        start(5, j, part.at[across, at, right], relay_down.at[at, :], below)

    def relay(j):
        at = packed_at(j)
        copies[4, j].wait_recv()
        part[above, at, left] = (part[above, at, left].astype(F32) + relay_up[at, :].astype(F32)).astype(BF16)
        start(6, j, part.at[above, at, :], from_down.at[at, :], above)
        copies[5, j].wait_recv()
        part[below, at, right] = (part[below, at, right].astype(F32) + relay_down[at, :].astype(F32)).astype(BF16)
        start(7, j, part.at[below, at, :], from_up.at[at, :], below)

    def send_back(j):
        at, wide = packed_at(j), padded_at(j)
        copies[6, j].wait_recv()
        copies[7, j].wait_recv()
        total = part[me, at, :].astype(F32) + from_down[at, :].astype(F32) + from_up[at, :].astype(F32)
        spread[wide, :] = dot(unpack[...], total.astype(BF16)).astype(BF16)
        if j == 0:
            back[own, :] = spread[own, :]

        @pl.loop(1 if j == 0 else 0, per)
        def _(i):
            to = block_of(j) * per + (my_place + i) % per
            exchange(spread, back, to, back_send, back_recv).start()

    stages = (gather_rows, forward_rows, compute, relay, send_back)
    delays = (0, 1, 2, 3, 4)
    for step in range(BLOCKS + delays[-1]):
        for stage, delay in zip(stages, delays):
            j = step - delay
            if 0 <= j < BLOCKS:
                if stage is compute and j == 0:
                    for load in loads:
                        load.wait()
                stage(j)

    others = pl.ds(0, (experts - 1) * SLOT)
    pltpu.make_async_copy(back.at[others, :], back.at[others, :], back_recv).wait()
    down_rows = (((0,), (0,)), ((), ()))
    mixed = lax.dot_general(mix_hi[...], back[...], down_rows, preferred_element_type=F32)
    out[...] = mixed + lax.dot_general(mix_lo[...], back[...], down_rows, preferred_element_type=F32)

    pltpu.make_async_copy(sent.at[others, :], sent.at[others, :], disp_send).wait()
    pltpu.make_async_copy(spread.at[others, :], spread.at[others, :], back_send).wait()
    for copy in copies.values():
        copy.wait_send()


def cold_experts(tokens, pick, mix_hi, mix_lo, w_gate, w_up, w_down):
    group_tok, width = tokens.shape
    experts, n_dp = lax.axis_size("expert"), lax.axis_size("dp")
    units, quarter, per = w_gate.shape[1], width // n_dp, experts // BLOCKS
    slots, held = experts * SLOT, experts * CAP
    block = per * CAP
    place = np.arange(block)
    wanted = (place // CAP) * SLOT + place % CAP
    pack = jnp.asarray(wanted[:, None] == np.arange(per * SLOT)[None, :], BF16)
    unpack = jnp.asarray(wanted[None, :] == np.arange(per * SLOT)[:, None], BF16)
    vmem, anywhere = pl.BlockSpec(memory_space=VMEM), pl.BlockSpec(memory_space=pl.ANY)
    dma = pltpu.SemaphoreType.DMA
    return pl.pallas_call(
        cold_kernel,
        name="cold_experts",
        out_shape=jax.ShapeDtypeStruct((group_tok, quarter), F32),
        in_specs=[vmem] * 6 + [anywhere] * 3,
        out_specs=vmem,
        scratch_shapes=[
            VMEM((slots, quarter), BF16),
            VMEM((slots, quarter), BF16),
            VMEM((n_dp, held, quarter), BF16),
            VMEM((n_dp, held, quarter), BF16),
            VMEM((held, quarter // 2), BF16),
            VMEM((held, quarter // 2), BF16),
            VMEM((held, quarter), BF16),
            VMEM((held, quarter), BF16),
            VMEM((slots, quarter), BF16),
            VMEM((slots, quarter), BF16),
            VMEM((width, units), BF16),
            VMEM((width, units), BF16),
            VMEM((units, width), BF16),
            VMEM((block, units), F32),
            VMEM((block, units), F32),
            dma((3,)),
            dma,
            dma((BLOCKS,)),
            dma((8, BLOCKS)),
            dma((8, BLOCKS)),
            dma,
            dma,
        ],
        compiler_params=pltpu.CompilerParams(vmem_limit_bytes=56 << 20, has_side_effects=True),
        cost_estimate=pl.CostEstimate(
            flops=6 * held * width * units, bytes_accessed=60 << 20, transcendentals=held * units
        ),
    )(tokens, pick, mix_hi, mix_lo, pack, unpack, w_gate, w_up, w_down)


def expert_partial(inputs, gate_mat, up_mat, down_mat):
    gate_val = jnp.dot(inputs, gate_mat, preferred_element_type=F32)
    up_val = jnp.dot(inputs, up_mat, preferred_element_type=F32)
    hidden = (jax.nn.silu(gate_val) * up_val).astype(BF16)
    return jnp.dot(hidden, down_mat, preferred_element_type=F32)


def split_weight(weight):
    high = lax.reduce_precision(weight, 8, 7)
    return high.astype(BF16), (weight - high).astype(BF16)


def local(tokens, routing, combine, w_gate, w_up, w_down):
    group_rows, chosen, mixing = tokens[0], routing[0], combine[0]
    w_gate, w_up, w_down = w_gate[0], w_up[0], w_down[0]
    group_tok = chosen.shape[0]
    experts = lax.axis_size("expert")
    ids = jnp.arange(experts, dtype=jnp.int32)
    hit = chosen.T[None, :, :] == ids[:, None, None]
    member = jnp.sum(hit.astype(F32), axis=1)
    weight = jnp.sum(jnp.where(hit, mixing.T[None, :, :], 0.0), axis=1)
    earlier = jnp.asarray(np.triu(np.ones((group_tok, group_tok)), 1), BF16)
    before = jnp.dot(member.astype(BF16), earlier, preferred_element_type=F32)
    hot_expert = jnp.argmax(jnp.sum(member, axis=1)).astype(jnp.int32)
    is_hot = (ids == hot_expert)[:, None]
    rank = jnp.where(member > 0, before, -1.0)

    picked = jnp.where(is_hot, -1.0, rank)[:, None, :] == jnp.arange(SLOT, dtype=F32)[None, :, None]
    high, low = split_weight(weight)
    zero = jnp.zeros((), BF16)
    pick = picked.astype(BF16).reshape(experts * SLOT, group_tok)
    mix_hi = jnp.where(picked, high[:, None, :], zero).reshape(experts * SLOT, group_tok)
    mix_lo = jnp.where(picked, low[:, None, :], zero).reshape(experts * SLOT, group_tok)

    hot_rank = jnp.sum(jnp.where(is_hot, rank, 0.0), axis=0)
    hot_weight = jnp.sum(jnp.where(is_hot, weight, 0.0), axis=0)
    hot_pick = hot_rank[None, :] == jnp.arange(HOT_CAP, dtype=F32)[:, None]

    owned = lax.axis_index("expert") == hot_expert
    hot_gate, hot_up, hot_down = lax.psum(
        tuple(jnp.where(owned, w, jnp.zeros_like(w)) for w in (w_gate, w_up, w_down)), "expert"
    )
    cold = cold_experts(group_rows, pick, mix_hi, mix_lo, w_gate, w_up, w_down)
    hot_pick, cold = lax.optimization_barrier((hot_pick, cold))
    hot_rows = jnp.dot(hot_pick.astype(BF16), group_rows, preferred_element_type=F32).astype(BF16)
    hot_part = expert_partial(hot_rows, hot_gate, hot_up, hot_down)
    hot_sum = lax.psum_scatter(hot_part.astype(BF16), "dp", scatter_dimension=1, tiled=True)
    hot_mix = jnp.where(hot_pick, hot_weight[None, :], 0.0)
    hot = lax.dot_general(
        hot_mix, hot_sum.astype(F32), (((0,), (0,)), ((), ())),
        precision=lax.Precision.HIGHEST, preferred_element_type=F32,
    )
    return (cold + hot).astype(BF16)[None]


def solution(mesh):
    placed = (
        P("expert", None, None),
        P("expert", None, None),
        P("expert", None, None),
        P("expert", None, "dp"),
        P("expert", None, "dp"),
        P("expert", "dp", None),
    )
    return jax.shard_map(
        local, mesh=mesh, in_specs=placed, out_specs=P("expert", None, "dp"), check_vma=False
    )
```

```python
import jax
import jax.numpy as jnp
import numpy as np
from jax import lax
from jax.experimental import pallas as pl
from jax.experimental.pallas import tpu as pltpu
from jax.sharding import PartitionSpec as P

CAP = 13
SLOT = 16
BLOCKS = 4
NX, NZ = 4, 8
HOT_ROWS = 48
MESH = pl.DeviceIdType.MESH
VMEM = pltpu.VMEM
BF16 = jnp.bfloat16
F32 = jnp.float32


def dot(a, b):
    return jnp.dot(a, b, preferred_element_type=F32)


def experts_kernel(
    owner, tok, pick, mix_hi, mix_lo, hot_pick, hot_hi, hot_lo, pack, unpack, gate_hbm, up_hbm, down_hbm, out,
    sent, got, rows, part, relay_up, relay_down, from_up, from_down, spread, back,
    w_gate, w_up, w_down, acc_gate, acc_up,
    hot_gate, hot_up, hot_down, half_gate, half_up, half_down, quarter_gate, quarter_up, quarter_down,
    kept_gate, kept_up, kept_down, piece_gate, piece_up, piece_down, hot_rows, hot_part, hot_got,
    load_sem, move_send, move_recv, hot_send, hot_recv, disp_send, disp_recv, y_send, y_recv, back_send, back_recv,
):
    n_dp, experts = rows.shape[0], got.shape[0] // SLOT
    per = experts // BLOCKS
    padded, packed = per * SLOT, per * CAP
    quarter = sent.shape[1]
    half = quarter // 2
    me, mine = lax.axis_index("dp"), lax.axis_index("expert")
    my_block, my_place = mine // per, mine % per
    above, below, across = (me + 1) % n_dp, (me + n_dp - 1) % n_dp, (me + 2) % n_dp

    x, z, core = mine // (2 * NZ), (mine // 2) % NZ, mine % 2
    given, held = (gate_hbm, up_hbm, down_hbm), (w_gate, w_up, w_down)
    loads = [pltpu.make_async_copy(src, dst, load_sem.at[i]) for i, (src, dst) in enumerate(zip(given, held))]
    for load in loads:
        load.start()

    full, halves = (hot_gate, hot_up, hot_down), (half_gate, half_up, half_down)
    quarters, kept = (quarter_gate, quarter_up, quarter_down), (kept_gate, kept_up, kept_down)
    pieces = (piece_gate, piece_up, piece_down)
    depth, units = w_gate.shape
    in_half, in_quarter, in_piece = depth // 2, depth // (2 * NX), depth // (2 * NX * NZ)

    def of_full(ref, t, lane, at, size):
        if t < 2:
            return ref.at[pl.ds(pl.multiple_of(lane * in_half + at, in_piece), size), :]
        rows_at = pl.ds(pl.multiple_of(lane * (units // 2), units // 2), units // 2)
        return ref.at[rows_at, pl.ds(pl.multiple_of(2 * at, 2 * in_piece), 2 * size)]

    def of_half(ref, t, at, size):
        if t < 2:
            return ref.at[pl.ds(pl.multiple_of(at, in_piece), size), :]
        return ref.at[:, pl.ds(pl.multiple_of(2 * at, 2 * in_piece), 2 * size)]

    def move(stage, t, src, dst, to):
        return pltpu.make_async_remote_copy(
            src_ref=src, dst_ref=dst, send_sem=move_send.at[stage, t], recv_sem=move_recv.at[stage, t],
            device_id={"expert": to}, device_id_type=MESH,
        )

    def moved_amount(stage, t):
        if stage in (0, 5):
            return halves[t]
        return quarters[t].at[pl.ds(0, NX - 1)] if stage in (1, 4) else pieces[t].at[pl.ds(0, NZ - 1)]

    def moved(stage, t, sems=move_recv):
        amount = moved_amount(stage, t)
        pltpu.make_async_copy(amount, amount, sems.at[stage, t]).wait()

    twin = mine + 1 - 2 * core

    def along_x(k):
        to = (x + k) % NX
        return to, (to * NZ + z) * 2 + core

    def along_z(k):
        to = (z + k) % NZ
        return to, (x * NZ + to) * 2 + core

    def swap_halves(t):
        move(0, t, of_full(given[t], t, 1 - core, 0, in_half), halves[t], twin).start()

    def scatter_x(t):
        loads[t].wait()
        moved(0, t)

        @pl.loop(0, 8)
        def _(i):
            here = of_half(halves[t], t, i * (in_half // 8), in_half // 8)
            ours = of_full(held[t], t, core, i * (in_half // 8), in_half // 8)
            here[...] = jnp.where(owner[2] == core, ours[...], here[...])

        for k in range(1, NX):
            to, device = along_x(k)
            move(1, t, of_half(halves[t], t, to * in_quarter, in_quarter), quarters[t].at[x], device).start()
        quarters[t][x] = of_half(halves[t], t, x * in_quarter, in_quarter)[...]

    def scatter_z(t):
        moved(1, t)
        kept[t][...] = quarters[t][owner[0]]

        @pl.loop(1, NZ)
        def _(k):
            to, device = along_z(k)
            move(2, t, of_half(kept[t], t, to * in_piece, in_piece), pieces[t].at[z], device).start()

        pieces[t][z] = of_half(kept[t], t, z * in_piece, in_piece)[...]

    def gather_z(t):
        moved(2, t)
        own_piece = of_full(full[t], t, core, x * in_quarter + z * in_piece, in_piece)
        own_piece[...] = pieces[t][owner[1]]

        @pl.loop(1, NZ)
        def _(k):
            move(3, t, own_piece, own_piece, along_z(k)[1]).start()

    def gather_x(t):
        moved(3, t)
        own_quarter = of_full(full[t], t, core, x * in_quarter, in_quarter)
        for k in range(1, NX):
            move(4, t, own_quarter, own_quarter, along_x(k)[1]).start()

    def join_halves(t):
        moved(4, t)
        own_half = of_full(full[t], t, core, 0, in_half)
        move(5, t, own_half, own_half, twin).start()

    for t in range(3):
        swap_halves(t)

    hot_at = pl.ds(0, HOT_ROWS)
    own_cols = pl.ds(pl.multiple_of(me * quarter, 128), quarter)

    @pl.loop(0, BLOCKS)
    def _(b):
        at = pl.ds(pl.multiple_of(b * padded, padded), padded)
        sent[at, :] = dot(pick[at, :], tok[:, own_cols]).astype(BF16)

    def slot(i):
        return pl.ds(pl.multiple_of(i * SLOT, SLOT), SLOT)

    own = slot(mine)
    got[own, :] = sent[own, :]

    def exchange(src, dst, to, send_sem, recv_sem):
        return pltpu.make_async_remote_copy(
            src_ref=src.at[slot(to), :], dst_ref=dst.at[own, :], send_sem=send_sem, recv_sem=recv_sem,
            device_id={"expert": to}, device_id_type=MESH,
        )

    for j in range(BLOCKS):

        @pl.loop(1 if j == 0 else 0, per)
        def _(i, j=j):
            to = ((my_block + j) % BLOCKS) * per + (my_place + i) % per
            exchange(sent, got, to, disp_send, disp_recv.at[j]).start()

    def hot_units():
        acc_gate[hot_at, :] = jnp.zeros((HOT_ROWS, units), F32)
        acc_up[hot_at, :] = jnp.zeros((HOT_ROWS, units), F32)
        moved(5, 0)
        moved(5, 1)

        @pl.loop(0, n_dp)
        def _(q):
            cols = pl.ds(pl.multiple_of(q * quarter, quarter), quarter)
            inputs = dot(hot_pick[...], tok[:, cols]).astype(BF16)
            acc_gate[hot_at, :] += dot(inputs, hot_gate[cols, :])
            acc_up[hot_at, :] += dot(inputs, hot_up[cols, :])

        hot_rows[...] = (jax.nn.silu(acc_gate[hot_at, :]) * acc_up[hot_at, :]).astype(BF16)

    def hot_results():
        moved(5, 2)

        @pl.loop(0, n_dp)
        def _(q):
            cols = pl.ds(pl.multiple_of(q * quarter, quarter), quarter)
            hot_part[q, :, :] = dot(hot_rows[...], hot_down[:, cols]).astype(BF16)

        for k in range(1, n_dp):
            hot_copy(k).start()

    def hot_copy(k):
        to = (me + k) % n_dp
        return pltpu.make_async_remote_copy(
            src_ref=hot_part.at[to], dst_ref=hot_got.at[k - 1], send_sem=hot_send.at[k - 1],
            recv_sem=hot_recv.at[k - 1], device_id={"dp": to}, device_id_type=MESH,
        )

    def across_dp(kind, j, src, dst, to):
        return pltpu.make_async_remote_copy(
            src_ref=src, dst_ref=dst, send_sem=y_send.at[kind, j], recv_sem=y_recv.at[kind, j],
            device_id={"dp": to}, device_id_type=MESH,
        )

    def block_of(j):
        return (my_block + BLOCKS - j) % BLOCKS

    def packed_at(j):
        return pl.ds(pl.multiple_of(block_of(j) * packed, 16), packed)

    def padded_at(j):
        return pl.ds(pl.multiple_of(block_of(j) * padded, padded), padded)

    left, right = pl.ds(0, half), pl.ds(half, half)
    copies = {}

    def start(kind, j, src, dst, to):
        copies[kind, j] = across_dp(kind, j, src, dst, to)
        copies[kind, j].start()

    def gather_rows(j):
        take = per - 1 if j == 0 else per
        pltpu.make_async_copy(
            got.at[pl.ds(0, take * SLOT), :], got.at[pl.ds(0, take * SLOT), :], disp_recv.at[j]
        ).wait()
        at = packed_at(j)
        rows[me, at, :] = dot(pack[...], got[padded_at(j), :]).astype(BF16)
        start(0, j, rows.at[me, at, :], rows.at[me, at, :], above)
        start(1, j, rows.at[me, at, :], rows.at[me, at, :], below)

    def forward_rows(j):
        at = packed_at(j)
        copies[0, j].wait_recv()
        start(2, j, rows.at[below, at, left], rows.at[below, at, left], above)
        copies[1, j].wait_recv()
        start(3, j, rows.at[above, at, right], rows.at[above, at, right], below)

    def compute(j):
        at = packed_at(j)
        copies[2, j].wait_recv()
        copies[3, j].wait_recv()
        acc_gate[...] = jnp.zeros_like(acc_gate)
        acc_up[...] = jnp.zeros_like(acc_up)

        @pl.loop(0, n_dp)
        def _(q):
            depth = pl.ds(pl.multiple_of(q * quarter, quarter), quarter)
            acc_gate[...] += dot(rows[q, at, :], w_gate[depth, :])
            acc_up[...] += dot(rows[q, at, :], w_up[depth, :])

        hidden = (jax.nn.silu(acc_gate[...]) * acc_up[...]).astype(BF16)

        @pl.loop(0, n_dp)
        def _(i):
            q = (across + i) % n_dp
            cols = pl.ds(pl.multiple_of(q * quarter, quarter), quarter)
            part[q, at, :] = dot(hidden, w_down[:, cols]).astype(BF16)

        start(4, j, part.at[across, at, left], relay_up.at[at, :], above)
        start(5, j, part.at[across, at, right], relay_down.at[at, :], below)

    def relay(j):
        at = packed_at(j)
        copies[4, j].wait_recv()
        part[above, at, left] = (part[above, at, left].astype(F32) + relay_up[at, :].astype(F32)).astype(BF16)
        start(6, j, part.at[above, at, :], from_down.at[at, :], above)
        copies[5, j].wait_recv()
        part[below, at, right] = (part[below, at, right].astype(F32) + relay_down[at, :].astype(F32)).astype(BF16)
        start(7, j, part.at[below, at, :], from_up.at[at, :], below)

    def send_back(j):
        at, wide = packed_at(j), padded_at(j)
        copies[6, j].wait_recv()
        copies[7, j].wait_recv()
        total = part[me, at, :].astype(F32) + from_down[at, :].astype(F32) + from_up[at, :].astype(F32)
        spread[wide, :] = dot(unpack[...], total.astype(BF16)).astype(BF16)
        if j == 0:
            back[own, :] = spread[own, :]

        @pl.loop(1 if j == 0 else 0, per)
        def _(i):
            to = block_of(j) * per + (my_place + i) % per
            exchange(spread, back, to, back_send, back_recv).start()

    stages = (gather_rows, forward_rows, compute, relay, send_back)
    delays = (0, 1, 2, 3, 4)
    moves = (scatter_x, scatter_z, gather_z, gather_x, join_halves)
    turns = (0, 1, 2, 3, 5)
    for t in range(3):
        scatter_x(t)
    for step in range(max(BLOCKS + delays[-1], 2 + turns[-1])):
        for stage, delay in zip(stages, delays):
            if 0 <= step - delay < BLOCKS:
                stage(step - delay)
        for stage, turn in zip(moves[1:], turns[1:]):
            t = step + 1 - turn
            if 0 <= t < 3:
                stage(t)
    hot_units()
    hot_results()

    others = pl.ds(0, (experts - 1) * SLOT)
    pltpu.make_async_copy(back.at[others, :], back.at[others, :], back_recv).wait()
    down_rows = (((0,), (0,)), ((), ()))
    mixed = lax.dot_general(mix_hi[...], back[...], down_rows, preferred_element_type=F32)
    mixed += lax.dot_general(mix_lo[...], back[...], down_rows, preferred_element_type=F32)
    hot_sum = hot_part[me, :, :].astype(F32)
    for k in range(1, n_dp):
        hot_copy(k).wait_recv()
        hot_sum += hot_got[k - 1, :, :].astype(F32)
    hot_sum = hot_sum.astype(BF16)
    mixed += lax.dot_general(hot_hi[...], hot_sum, down_rows, preferred_element_type=F32)
    mixed += lax.dot_general(hot_lo[...], hot_sum, down_rows, preferred_element_type=F32)
    out[...] = mixed.astype(BF16)

    pltpu.make_async_copy(sent.at[others, :], sent.at[others, :], disp_send).wait()
    pltpu.make_async_copy(spread.at[others, :], spread.at[others, :], back_send).wait()
    for copy in copies.values():
        copy.wait_send()
    for k in range(1, n_dp):
        hot_copy(k).wait_send()
    for t in range(3):
        for stage in range(6):
            moved(stage, t, move_send)


def routed_experts(owner, tokens, pick, mix_hi, mix_lo, hot_pick, hot_hi, hot_lo, weights):
    group_tok, width = tokens.shape
    experts, n_dp = lax.axis_size("expert"), lax.axis_size("dp")
    units, quarter, per = weights[0].shape[1], width // n_dp, experts // BLOCKS
    slots, held = experts * SLOT, experts * CAP
    block = per * CAP
    kept, kept_down = (width // (2 * NX), units), (units // 2, width // NX)
    piece, piece_down = (kept[0] // NZ, units), (units // 2, kept_down[1] // NZ)
    place = np.arange(block)
    wanted = (place // CAP) * SLOT + place % CAP
    pack = jnp.asarray(wanted[:, None] == np.arange(per * SLOT)[None, :], BF16)
    unpack = jnp.asarray(wanted[None, :] == np.arange(per * SLOT)[:, None], BF16)
    vmem, anywhere = pl.BlockSpec(memory_space=VMEM), pl.BlockSpec(memory_space=pl.ANY)
    dma = pltpu.SemaphoreType.DMA
    return pl.pallas_call(
        experts_kernel,
        name="routed_experts",
        out_shape=jax.ShapeDtypeStruct((group_tok, quarter), BF16),
        in_specs=[pl.BlockSpec(memory_space=pltpu.SMEM)] + [vmem] * 9 + [anywhere] * 3,
        out_specs=vmem,
        scratch_shapes=[
            VMEM((slots, quarter), BF16),
            VMEM((slots, quarter), BF16),
            VMEM((n_dp, held, quarter), BF16),
            VMEM((n_dp, held, quarter), BF16),
            VMEM((held, quarter // 2), BF16),
            VMEM((held, quarter // 2), BF16),
            VMEM((held, quarter), BF16),
            VMEM((held, quarter), BF16),
            VMEM((slots, quarter), BF16),
            VMEM((slots, quarter), BF16),
            VMEM((width, units), BF16),
            VMEM((width, units), BF16),
            VMEM((units, width), BF16),
            VMEM((block, units), F32),
            VMEM((block, units), F32),
            VMEM((width, units), BF16),
            VMEM((width, units), BF16),
            VMEM((units, width), BF16),
            *[VMEM(shape, BF16) for shape in ((width // 2, units), (width // 2, units), (units // 2, width))],
            *[VMEM((NX, *shape), BF16) for shape in (kept, kept, kept_down)],
            *[VMEM(shape, BF16) for shape in (kept, kept, kept_down)],
            *[VMEM((NZ, *shape), BF16) for shape in (piece, piece, piece_down)],
            VMEM((HOT_ROWS, units), BF16),
            VMEM((n_dp, HOT_ROWS, quarter), BF16),
            VMEM((n_dp - 1, HOT_ROWS, quarter), BF16),
            dma((3,)),
            dma((6, 3)),
            dma((6, 3)),
            dma((n_dp - 1,)),
            dma((n_dp - 1,)),
            dma,
            dma((BLOCKS,)),
            dma((8, BLOCKS)),
            dma((8, BLOCKS)),
            dma,
            dma,
        ],
        compiler_params=pltpu.CompilerParams(vmem_limit_bytes=63 << 20, has_side_effects=True),
        cost_estimate=pl.CostEstimate(
            flops=6 * held * width * units, bytes_accessed=60 << 20, transcendentals=held * units
        ),
    )(owner, tokens, pick, mix_hi, mix_lo, hot_pick, hot_hi, hot_lo, pack, unpack, *weights)


def split_weight(weight):
    high = lax.reduce_precision(weight, 8, 7)
    return high.astype(BF16), (weight - high).astype(BF16)


def local(tokens, routing, combine, w_gate, w_up, w_down):
    group_rows, chosen, mixing = tokens[0], routing[0], combine[0]
    w_gate, w_up, w_down = w_gate[0], w_up[0], w_down[0]
    group_tok = chosen.shape[0]
    experts = lax.axis_size("expert")
    ids = jnp.arange(experts, dtype=jnp.int32)
    hit = chosen.T[None, :, :] == ids[:, None, None]
    member = jnp.sum(hit.astype(F32), axis=1)
    weight = jnp.sum(jnp.where(hit, mixing.T[None, :, :], 0.0), axis=1)
    earlier = jnp.asarray(np.triu(np.ones((group_tok, group_tok)), 1), BF16)
    before = jnp.dot(member.astype(BF16), earlier, preferred_element_type=F32)
    hot_expert = jnp.argmax(jnp.sum(member, axis=1)).astype(jnp.int32)
    is_hot = (ids == hot_expert)[:, None]
    rank = jnp.where(member > 0, before, -1.0)

    picked = jnp.where(is_hot, -1.0, rank)[:, None, :] == jnp.arange(SLOT, dtype=F32)[None, :, None]
    high, low = split_weight(weight)
    zero = jnp.zeros((), BF16)
    pick = picked.astype(BF16).reshape(experts * SLOT, group_tok)
    mix_hi = jnp.where(picked, high[:, None, :], zero).reshape(experts * SLOT, group_tok)
    mix_lo = jnp.where(picked, low[:, None, :], zero).reshape(experts * SLOT, group_tok)

    hot_rank = jnp.sum(jnp.where(is_hot, rank, 0.0), axis=0)
    hot_weight = jnp.sum(jnp.where(is_hot, weight, 0.0), axis=0)
    hot_picked = hot_rank[None, :] == jnp.arange(HOT_ROWS, dtype=F32)[:, None]
    hot_high, hot_low = split_weight(hot_weight)
    hot_pick = hot_picked.astype(BF16)
    hot_hi = jnp.where(hot_picked, hot_high[None, :], zero)
    hot_lo = jnp.where(hot_picked, hot_low[None, :], zero)

    weights = (w_gate, w_up, w_down)
    owner = jnp.stack([hot_expert // (2 * NZ), (hot_expert // 2) % NZ, hot_expert % 2])
    mixed = routed_experts(owner, group_rows, pick, mix_hi, mix_lo, hot_pick, hot_hi, hot_lo, weights)
    return mixed[None]


def solution(mesh):
    placed = (
        P("expert", None, None),
        P("expert", None, None),
        P("expert", None, None),
        P("expert", None, "dp"),
        P("expert", None, "dp"),
        P("expert", "dp", None),
    )
    return jax.shard_map(
        local, mesh=mesh, in_specs=placed, out_specs=P("expert", None, "dp"), check_vma=False
    )
```

```python
import jax
import jax.numpy as jnp
import numpy as np
from jax import lax
from jax.experimental import pallas as pl
from jax.experimental.pallas import tpu as pltpu
from jax.sharding import PartitionSpec as P

CAP = 13
SLOT = 16
BLOCKS = 4
NX, NZ = 4, 8
HOT_ROWS = 48
MESH = pl.DeviceIdType.MESH
VMEM = pltpu.VMEM
BF16 = jnp.bfloat16
F32 = jnp.float32


def dot(a, b):
    return jnp.dot(a, b, preferred_element_type=F32)


def experts_kernel(
    tok, chosen, mixing, pack, unpack, gate_hbm, up_hbm, down_hbm, out,
    mix_hi, mix_lo, hot_pick, hot_hi, hot_lo,
    sent, got, rows, part, relay_up, relay_down, from_up, from_down, spread, back,
    w_gate, w_up, w_down, acc_gate, acc_up,
    hot_gate, hot_up, hot_down, half_gate, half_up, half_down, quarter_gate, quarter_up, quarter_down,
    kept_gate, kept_up, kept_down, piece_gate, piece_up, piece_down, hot_rows, hot_part, hot_got,
    load_sem, move_send, move_recv, hot_send, hot_recv, disp_send, disp_recv, y_send, y_recv, back_send, back_recv,
):
    n_dp, experts = rows.shape[0], got.shape[0] // SLOT
    per = experts // BLOCKS
    padded, packed = per * SLOT, per * CAP
    quarter = sent.shape[1]
    half = quarter // 2
    me, mine = lax.axis_index("dp"), lax.axis_index("expert")
    my_block, my_place = mine // per, mine % per
    above, below, across = (me + 1) % n_dp, (me + n_dp - 1) % n_dp, (me + 2) % n_dp

    barrier = pltpu.get_barrier_semaphore()

    @pl.loop(1, experts)
    def _(k):
        pl.semaphore_signal(barrier, inc=1, device_id={"expert": (mine + k) % experts}, device_id_type=MESH)

    for k in range(1, n_dp):
        pl.semaphore_signal(barrier, inc=1, device_id={"dp": (me + k) % n_dp}, device_id_type=MESH)

    x, z, core = mine // (2 * NZ), (mine // 2) % NZ, mine % 2
    given, held = (gate_hbm, up_hbm, down_hbm), (w_gate, w_up, w_down)
    loads = [pltpu.make_async_copy(src, dst, load_sem.at[i]) for i, (src, dst) in enumerate(zip(given, held))]
    for load in loads:
        load.start()

    full, halves = (hot_gate, hot_up, hot_down), (half_gate, half_up, half_down)
    quarters, kept = (quarter_gate, quarter_up, quarter_down), (kept_gate, kept_up, kept_down)
    pieces = (piece_gate, piece_up, piece_down)
    depth, units = w_gate.shape
    in_half, in_quarter, in_piece = depth // 2, depth // (2 * NX), depth // (2 * NX * NZ)

    def of_full(ref, t, lane, at, size):
        if t < 2:
            return ref.at[pl.ds(pl.multiple_of(lane * in_half + at, in_piece), size), :]
        rows_at = pl.ds(pl.multiple_of(lane * (units // 2), units // 2), units // 2)
        return ref.at[rows_at, pl.ds(pl.multiple_of(2 * at, 2 * in_piece), 2 * size)]

    def of_half(ref, t, at, size):
        if t < 2:
            return ref.at[pl.ds(pl.multiple_of(at, in_piece), size), :]
        return ref.at[:, pl.ds(pl.multiple_of(2 * at, 2 * in_piece), 2 * size)]

    def move(stage, t, src, dst, to):
        return pltpu.make_async_remote_copy(
            src_ref=src, dst_ref=dst, send_sem=move_send.at[stage, t], recv_sem=move_recv.at[stage, t],
            device_id={"expert": to}, device_id_type=MESH,
        )

    def moved_amount(stage, t):
        if stage in (0, 5):
            return halves[t]
        return quarters[t].at[pl.ds(0, NX - 1)] if stage in (1, 4) else pieces[t].at[pl.ds(0, NZ - 1)]

    def moved(stage, t, sems=move_recv):
        amount = moved_amount(stage, t)
        pltpu.make_async_copy(amount, amount, sems.at[stage, t]).wait()

    twin = mine + 1 - 2 * core

    def along_x(k):
        to = (x + k) % NX
        return to, (to * NZ + z) * 2 + core

    def along_z(k):
        to = (z + k) % NZ
        return to, (x * NZ + to) * 2 + core

    def swap_halves(t):
        move(0, t, of_full(given[t], t, 1 - core, 0, in_half), halves[t], twin).start()

    def scatter_x(t):
        loads[t].wait()
        moved(0, t)

        @pl.loop(0, 8)
        def _(i):
            here = of_half(halves[t], t, i * (in_half // 8), in_half // 8)
            ours = of_full(held[t], t, core, i * (in_half // 8), in_half // 8)
            here[...] = ours[...] * matches(owner_core, core) + here[...] * matches(owner_core, 1 - core)

        for k in range(1, NX):
            to, device = along_x(k)
            move(1, t, of_half(halves[t], t, to * in_quarter, in_quarter), quarters[t].at[x], device).start()
        quarters[t][x] = of_half(halves[t], t, x * in_quarter, in_quarter)[...]

    def scatter_z(t):
        moved(1, t)
        kept[t][...] = sum(quarters[t][i] * matches(owner_x, i) for i in range(NX))

        @pl.loop(1, NZ)
        def _(k):
            to, device = along_z(k)
            move(2, t, of_half(kept[t], t, to * in_piece, in_piece), pieces[t].at[z], device).start()

        pieces[t][z] = of_half(kept[t], t, z * in_piece, in_piece)[...]

    def gather_z(t):
        moved(2, t)
        own_piece = of_full(full[t], t, core, x * in_quarter + z * in_piece, in_piece)
        own_piece[...] = sum(pieces[t][i] * matches(owner_z, i) for i in range(NZ))

        @pl.loop(1, NZ)
        def _(k):
            move(3, t, own_piece, own_piece, along_z(k)[1]).start()

    def gather_x(t):
        moved(3, t)
        own_quarter = of_full(full[t], t, core, x * in_quarter, in_quarter)
        for k in range(1, NX):
            move(4, t, own_quarter, own_quarter, along_x(k)[1]).start()

    def join_halves(t):
        moved(4, t)
        own_half = of_full(full[t], t, core, 0, in_half)
        move(5, t, own_half, own_half, twin).start()

    hot_at = pl.ds(0, HOT_ROWS)
    own_cols = pl.ds(pl.multiple_of(me * quarter, 128), quarter)
    group_tok, top = chosen.shape
    first_rows = (((0,), (0,)), ((), ()))

    def count(shape, axis):
        return lax.broadcasted_iota(jnp.int32, shape, axis)

    def as_ones(mask):
        return jnp.where(mask, 1.0, 0.0).astype(BF16)

    def turned(value):
        size = value.shape[0]
        eye = as_ones(count((size, size), 0) == count((size, size), 1))
        return lax.dot_general(value.astype(BF16), eye, first_rows, preferred_element_type=F32)

    high = mixing[...].astype(BF16)
    low = (mixing[...] - high.astype(F32)).astype(BF16)
    ids, high, low = turned(chosen[...].astype(F32)), turned(high), turned(low)
    expert = count((experts, group_tok), 0).astype(F32)
    member, weight_hi, weight_lo = (jnp.zeros((experts, group_tok), F32) for _ in range(3))
    for k in range(top):
        hit = ids[k : k + 1, :] == expert
        member += jnp.where(hit, 1.0, 0.0)
        weight_hi += jnp.where(hit, high[k : k + 1, :], 0.0)
        weight_lo += jnp.where(hit, low[k : k + 1, :], 0.0)
    earlier = as_ones(count((group_tok, group_tok), 0) < count((group_tok, group_tok), 1))
    rank = jnp.where(member > 0.0, dot(member.astype(BF16), earlier), -1.0)
    picks = jnp.sum(member, axis=1, keepdims=True)
    is_hot = picks == jnp.max(picks, axis=0, keepdims=True)
    cold_rank = jnp.where(is_hot, -1.0, rank)

    def of_hot(value):
        return jnp.sum(jnp.where(is_hot, value, 0.0), axis=0, keepdims=True)

    place = count((experts, 1), 0)
    z_bits = NZ.bit_length() - 1
    owner_core = of_hot((place & 1).astype(F32))
    owner_z = of_hot((lax.shift_right_logical(place, 1) & (NZ - 1)).astype(F32))
    owner_x = of_hot(lax.shift_right_logical(place, 1 + z_bits).astype(F32))

    def matches(value, index):
        return as_ones(value == jnp.asarray(index).astype(F32))

    hot_picked = of_hot(rank) == count((HOT_ROWS, group_tok), 0).astype(F32)
    hot_pick[...] = as_ones(hot_picked)
    hot_hi[...] = jnp.where(hot_picked, of_hot(weight_hi), 0.0).astype(BF16)
    hot_lo[...] = jnp.where(hot_picked, of_hot(weight_lo), 0.0).astype(BF16)

    def belongs(slot_at, expert_at):
        return as_ones(jnp.logical_and(slot_at >= expert_at * SLOT, slot_at < (expert_at + 1) * SLOT))

    @pl.loop(0, BLOCKS)
    def _(b):
        at = pl.ds(pl.multiple_of(b * padded, padded), padded)
        spread_out = belongs(count((padded, experts), 0) + b * padded, count((padded, experts), 1))
        slots = (count((padded, group_tok), 0) & (SLOT - 1)).astype(F32)
        pick = as_ones(dot(spread_out, cold_rank.astype(BF16)) == slots)
        sent[at, :] = dot(pick, tok[:, own_cols]).astype(BF16)

    def mixing_tables():
        by_token = [turned(value).astype(BF16) for value in (cold_rank, weight_hi, weight_lo)]

        @pl.loop(0, BLOCKS)
        def _(b):
            at = pl.ds(pl.multiple_of(b * padded, padded), padded)
            spread_out = belongs(count((experts, padded), 1) + b * padded, count((experts, padded), 0))
            slots = (count((group_tok, padded), 1) & (SLOT - 1)).astype(F32)
            picked = dot(by_token[0], spread_out) == slots
            mix_hi[:, at] = jnp.where(picked, dot(by_token[1], spread_out), 0.0).astype(BF16)
            mix_lo[:, at] = jnp.where(picked, dot(by_token[2], spread_out), 0.0).astype(BF16)

    pl.semaphore_wait(barrier, experts - 1 + n_dp - 1)

    def slot(i):
        return pl.ds(pl.multiple_of(i * SLOT, SLOT), SLOT)

    own = slot(mine)
    got[own, :] = sent[own, :]

    def exchange(src, dst, to, send_sem, recv_sem):
        return pltpu.make_async_remote_copy(
            src_ref=src.at[slot(to), :], dst_ref=dst.at[own, :], send_sem=send_sem, recv_sem=recv_sem,
            device_id={"expert": to}, device_id_type=MESH,
        )

    for j in range(BLOCKS):

        @pl.loop(1 if j == 0 else 0, per)
        def _(i, j=j):
            to = ((my_block + j) % BLOCKS) * per + (my_place + i) % per
            exchange(sent, got, to, disp_send, disp_recv.at[j]).start()

    for t in range(3):
        swap_halves(t)
    mixing_tables()

    def hot_units():
        acc_gate[hot_at, :] = jnp.zeros((HOT_ROWS, units), F32)
        acc_up[hot_at, :] = jnp.zeros((HOT_ROWS, units), F32)
        moved(5, 0)
        moved(5, 1)

        @pl.loop(0, n_dp)
        def _(q):
            cols = pl.ds(pl.multiple_of(q * quarter, quarter), quarter)
            inputs = dot(hot_pick[...], tok[:, cols]).astype(BF16)
            acc_gate[hot_at, :] += dot(inputs, hot_gate[cols, :])
            acc_up[hot_at, :] += dot(inputs, hot_up[cols, :])

        hot_rows[...] = (jax.nn.silu(acc_gate[hot_at, :]) * acc_up[hot_at, :]).astype(BF16)

    def hot_results():
        moved(5, 2)

        @pl.loop(0, n_dp)
        def _(q):
            cols = pl.ds(pl.multiple_of(q * quarter, quarter), quarter)
            hot_part[q, :, :] = dot(hot_rows[...], hot_down[:, cols]).astype(BF16)

        for k in range(1, n_dp):
            hot_copy(k).start()

    def hot_copy(k):
        to = (me + k) % n_dp
        return pltpu.make_async_remote_copy(
            src_ref=hot_part.at[to], dst_ref=hot_got.at[k - 1], send_sem=hot_send.at[k - 1],
            recv_sem=hot_recv.at[k - 1], device_id={"dp": to}, device_id_type=MESH,
        )

    def across_dp(kind, j, src, dst, to):
        return pltpu.make_async_remote_copy(
            src_ref=src, dst_ref=dst, send_sem=y_send.at[kind, j], recv_sem=y_recv.at[kind, j],
            device_id={"dp": to}, device_id_type=MESH,
        )

    def block_of(j):
        return (my_block + BLOCKS - j) % BLOCKS

    def packed_at(j):
        return pl.ds(pl.multiple_of(block_of(j) * packed, 16), packed)

    def padded_at(j):
        return pl.ds(pl.multiple_of(block_of(j) * padded, padded), padded)

    left, right = pl.ds(0, half), pl.ds(half, half)
    copies = {}

    def start(kind, j, src, dst, to):
        copies[kind, j] = across_dp(kind, j, src, dst, to)
        copies[kind, j].start()

    def gather_rows(j):
        take = per - 1 if j == 0 else per
        pltpu.make_async_copy(
            got.at[pl.ds(0, take * SLOT), :], got.at[pl.ds(0, take * SLOT), :], disp_recv.at[j]
        ).wait()
        at = packed_at(j)
        rows[me, at, :] = dot(pack[...], got[padded_at(j), :]).astype(BF16)
        start(0, j, rows.at[me, at, :], rows.at[me, at, :], above)
        start(1, j, rows.at[me, at, :], rows.at[me, at, :], below)

    def forward_rows(j):
        at = packed_at(j)
        copies[0, j].wait_recv()
        start(2, j, rows.at[below, at, left], rows.at[below, at, left], above)
        copies[1, j].wait_recv()
        start(3, j, rows.at[above, at, right], rows.at[above, at, right], below)

    def compute(j):
        at = packed_at(j)
        copies[2, j].wait_recv()
        copies[3, j].wait_recv()
        acc_gate[...] = jnp.zeros_like(acc_gate)
        acc_up[...] = jnp.zeros_like(acc_up)

        @pl.loop(0, n_dp)
        def _(q):
            depth = pl.ds(pl.multiple_of(q * quarter, quarter), quarter)
            acc_gate[...] += dot(rows[q, at, :], w_gate[depth, :])
            acc_up[...] += dot(rows[q, at, :], w_up[depth, :])

        hidden = (jax.nn.silu(acc_gate[...]) * acc_up[...]).astype(BF16)

        @pl.loop(0, n_dp)
        def _(i):
            q = (across + i) % n_dp
            cols = pl.ds(pl.multiple_of(q * quarter, quarter), quarter)
            part[q, at, :] = dot(hidden, w_down[:, cols]).astype(BF16)

        start(4, j, part.at[across, at, left], relay_up.at[at, :], above)
        start(5, j, part.at[across, at, right], relay_down.at[at, :], below)

    def relay(j):
        at = packed_at(j)
        copies[4, j].wait_recv()
        part[above, at, left] = (part[above, at, left].astype(F32) + relay_up[at, :].astype(F32)).astype(BF16)
        start(6, j, part.at[above, at, :], from_down.at[at, :], above)
        copies[5, j].wait_recv()
        part[below, at, right] = (part[below, at, right].astype(F32) + relay_down[at, :].astype(F32)).astype(BF16)
        start(7, j, part.at[below, at, :], from_up.at[at, :], below)

    def send_back(j):
        at, wide = packed_at(j), padded_at(j)
        copies[6, j].wait_recv()
        copies[7, j].wait_recv()
        total = part[me, at, :].astype(F32) + from_down[at, :].astype(F32) + from_up[at, :].astype(F32)
        spread[wide, :] = dot(unpack[...], total.astype(BF16)).astype(BF16)
        if j == 0:
            back[own, :] = spread[own, :]

        @pl.loop(1 if j == 0 else 0, per)
        def _(i):
            to = block_of(j) * per + (my_place + i) % per
            exchange(spread, back, to, back_send, back_recv).start()

    stages = (gather_rows, forward_rows, compute, relay, send_back)
    delays = (0, 1, 2, 3, 4)
    moves = (scatter_x, scatter_z, gather_z, gather_x, join_halves)
    turns = (0, 1, 2, 3, 5)
    for t in range(3):
        scatter_x(t)
    for step in range(max(BLOCKS + delays[-1], 2 + turns[-1])):
        for stage, delay in zip(stages, delays):
            if 0 <= step - delay < BLOCKS:
                stage(step - delay)
        for stage, turn in zip(moves[1:], turns[1:]):
            t = step + 1 - turn
            if 0 <= t < 3:
                stage(t)
    hot_units()
    hot_results()

    others = pl.ds(0, (experts - 1) * SLOT)
    pltpu.make_async_copy(back.at[others, :], back.at[others, :], back_recv).wait()
    mixed = dot(mix_hi[...], back[...]) + dot(mix_lo[...], back[...])
    hot_sum = hot_part[me, :, :].astype(F32)
    for k in range(1, n_dp):
        hot_copy(k).wait_recv()
        hot_sum += hot_got[k - 1, :, :].astype(F32)
    hot_sum = hot_sum.astype(BF16)
    mixed += lax.dot_general(hot_hi[...], hot_sum, first_rows, preferred_element_type=F32)
    mixed += lax.dot_general(hot_lo[...], hot_sum, first_rows, preferred_element_type=F32)
    out[...] = mixed.astype(BF16)

    pltpu.make_async_copy(sent.at[others, :], sent.at[others, :], disp_send).wait()
    pltpu.make_async_copy(spread.at[others, :], spread.at[others, :], back_send).wait()
    for copy in copies.values():
        copy.wait_send()
    for k in range(1, n_dp):
        hot_copy(k).wait_send()
    for t in range(3):
        for stage in range(6):
            moved(stage, t, move_send)


def local(tokens, routing, combine, *weights):
    tokens, routing, combine = tokens[0], routing[0], combine[0]
    weights = [weight[0] for weight in weights]
    group_tok, width = tokens.shape
    experts, n_dp = lax.axis_size("expert"), lax.axis_size("dp")
    units, quarter, per = weights[0].shape[1], width // n_dp, experts // BLOCKS
    slots, held = experts * SLOT, experts * CAP
    block = per * CAP
    kept, kept_down = (width // (2 * NX), units), (units // 2, width // NX)
    piece, piece_down = (kept[0] // NZ, units), (units // 2, kept_down[1] // NZ)
    place = np.arange(block)
    wanted = (place // CAP) * SLOT + place % CAP
    pack = jnp.asarray(wanted[:, None] == np.arange(per * SLOT)[None, :], BF16)
    unpack = jnp.asarray(wanted[None, :] == np.arange(per * SLOT)[:, None], BF16)
    vmem, anywhere = pl.BlockSpec(memory_space=VMEM), pl.BlockSpec(memory_space=pl.ANY)
    dma = pltpu.SemaphoreType.DMA
    mixed = pl.pallas_call(
        experts_kernel,
        name="routed_experts",
        out_shape=jax.ShapeDtypeStruct((group_tok, quarter), BF16),
        in_specs=[vmem] * 5 + [anywhere] * 3,
        out_specs=vmem,
        scratch_shapes=[
            VMEM((group_tok, slots), BF16),
            VMEM((group_tok, slots), BF16),
            *[VMEM((HOT_ROWS, group_tok), BF16)] * 3,
            VMEM((slots, quarter), BF16),
            VMEM((slots, quarter), BF16),
            VMEM((n_dp, held, quarter), BF16),
            VMEM((n_dp, held, quarter), BF16),
            VMEM((held, quarter // 2), BF16),
            VMEM((held, quarter // 2), BF16),
            VMEM((held, quarter), BF16),
            VMEM((held, quarter), BF16),
            VMEM((slots, quarter), BF16),
            VMEM((slots, quarter), BF16),
            VMEM((width, units), BF16),
            VMEM((width, units), BF16),
            VMEM((units, width), BF16),
            VMEM((block, units), F32),
            VMEM((block, units), F32),
            VMEM((width, units), BF16),
            VMEM((width, units), BF16),
            VMEM((units, width), BF16),
            *[VMEM(shape, BF16) for shape in ((width // 2, units), (width // 2, units), (units // 2, width))],
            *[VMEM((NX, *shape), BF16) for shape in (kept, kept, kept_down)],
            *[VMEM(shape, BF16) for shape in (kept, kept, kept_down)],
            *[VMEM((NZ, *shape), BF16) for shape in (piece, piece, piece_down)],
            VMEM((HOT_ROWS, units), BF16),
            VMEM((n_dp, HOT_ROWS, quarter), BF16),
            VMEM((n_dp - 1, HOT_ROWS, quarter), BF16),
            dma((3,)),
            dma((6, 3)),
            dma((6, 3)),
            dma((n_dp - 1,)),
            dma((n_dp - 1,)),
            dma,
            dma((BLOCKS,)),
            dma((8, BLOCKS)),
            dma((8, BLOCKS)),
            dma,
            dma,
        ],
        compiler_params=pltpu.CompilerParams(vmem_limit_bytes=63 << 20, has_side_effects=True, collective_id=0),
        cost_estimate=pl.CostEstimate(
            flops=6 * held * width * units, bytes_accessed=60 << 20, transcendentals=held * units
        ),
    )(tokens, routing, combine, pack, unpack, *weights)
    return mixed[None]


def solution(mesh):
    placed = (
        P("expert", None, None),
        P("expert", None, None),
        P("expert", None, None),
        P("expert", None, "dp"),
        P("expert", None, "dp"),
        P("expert", "dp", None),
    )
    return jax.shard_map(
        local, mesh=mesh, in_specs=placed, out_specs=P("expert", None, "dp"), check_vma=False
    )
```

```python
import jax
import jax.numpy as jnp
import numpy as np
from jax import lax
from jax.experimental import pallas as pl
from jax.experimental.pallas import tpu as pltpu
from jax.sharding import PartitionSpec as P

CAP = 13
SLOT = 16
BLOCKS = 4
NX, NZ = 4, 8
HOT_ROWS = 48
MESH = pl.DeviceIdType.MESH
VMEM = pltpu.VMEM
BF16 = jnp.bfloat16
F32 = jnp.float32


def dot(a, b):
    return jnp.dot(a, b, preferred_element_type=F32)


def experts_kernel(
    tok, chosen, mixing, pack, unpack, gate_hbm, up_hbm, down_hbm, out,
    mix_hi, mix_lo, hot_pick, hot_hi, hot_lo,
    sent, got, rows, part, relay_up, relay_down, from_up, from_down, spread, back,
    w_gate, w_up, w_down, acc_gate, acc_up,
    hot_gate, hot_up, hot_down, half_gate, half_up, half_down, quarter_gate, quarter_up, quarter_down,
    kept_gate, kept_up, kept_down, piece_gate, piece_up, piece_down, hot_rows, hot_part, hot_got,
    load_sem, move_send, move_recv, hot_send, hot_recv, disp_send, disp_recv, y_send, y_recv, back_send, back_recv,
):
    n_dp, experts = rows.shape[0], got.shape[0] // SLOT
    per = experts // BLOCKS
    padded, packed = per * SLOT, per * CAP
    quarter = sent.shape[1]
    half = quarter // 2
    me, mine = lax.axis_index("dp"), lax.axis_index("expert")
    my_block, my_place = mine // per, mine % per
    above, below, across = (me + 1) % n_dp, (me + n_dp - 1) % n_dp, (me + 2) % n_dp

    barrier = pltpu.get_barrier_semaphore()

    @pl.loop(1, experts)
    def _(k):
        pl.semaphore_signal(barrier, inc=1, device_id={"expert": (mine + k) % experts}, device_id_type=MESH)

    for k in range(1, n_dp):
        pl.semaphore_signal(barrier, inc=1, device_id={"dp": (me + k) % n_dp}, device_id_type=MESH)

    x, z, core = mine // (2 * NZ), (mine // 2) % NZ, mine % 2
    given, held = (gate_hbm, up_hbm, down_hbm), (w_gate, w_up, w_down)
    loads = [pltpu.make_async_copy(src, dst, load_sem.at[i]) for i, (src, dst) in enumerate(zip(given, held))]
    for load in loads:
        load.start()

    full, halves = (hot_gate, hot_up, hot_down), (half_gate, half_up, half_down)
    quarters, kept = (quarter_gate, quarter_up, quarter_down), (kept_gate, kept_up, kept_down)
    pieces = (piece_gate, piece_up, piece_down)
    depth, units = w_gate.shape
    in_half, in_quarter, in_piece = depth // 2, depth // (2 * NX), depth // (2 * NX * NZ)

    def of_full(ref, t, lane, at, size):
        if t < 2:
            return ref.at[pl.ds(pl.multiple_of(lane * in_half + at, in_piece), size), :]
        rows_at = pl.ds(pl.multiple_of(lane * (units // 2), units // 2), units // 2)
        return ref.at[rows_at, pl.ds(pl.multiple_of(2 * at, 2 * in_piece), 2 * size)]

    def of_half(ref, t, at, size):
        if t < 2:
            return ref.at[pl.ds(pl.multiple_of(at, in_piece), size), :]
        return ref.at[:, pl.ds(pl.multiple_of(2 * at, 2 * in_piece), 2 * size)]

    def move(stage, t, src, dst, to):
        return pltpu.make_async_remote_copy(
            src_ref=src, dst_ref=dst, send_sem=move_send.at[stage, t], recv_sem=move_recv.at[stage, t],
            device_id={"expert": to}, device_id_type=MESH,
        )

    def moved_amount(stage, t):
        if stage in (0, 5):
            return halves[t]
        return quarters[t].at[pl.ds(0, NX - 1)] if stage in (1, 4) else pieces[t].at[pl.ds(0, NZ - 1)]

    def moved(stage, t, sems=move_recv):
        amount = moved_amount(stage, t)
        pltpu.make_async_copy(amount, amount, sems.at[stage, t]).wait()

    twin = mine + 1 - 2 * core

    def along_x(k):
        to = (x + k) % NX
        return to, (to * NZ + z) * 2 + core

    def along_z(k):
        to = (z + k) % NZ
        return to, (x * NZ + to) * 2 + core

    def swap_halves(t):
        move(0, t, of_full(given[t], t, 1 - core, 0, in_half), halves[t], twin).start()

    def scatter_x(t):
        loads[t].wait()
        moved(0, t)

        @pl.loop(0, 8)
        def _(i):
            here = of_half(halves[t], t, i * (in_half // 8), in_half // 8)
            ours = of_full(held[t], t, core, i * (in_half // 8), in_half // 8)
            here[...] = ours[...] * matches(owner_core, core) + here[...] * matches(owner_core, 1 - core)

        for k in range(1, NX):
            to, device = along_x(k)
            move(1, t, of_half(halves[t], t, to * in_quarter, in_quarter), quarters[t].at[x], device).start()
        quarters[t][x] = of_half(halves[t], t, x * in_quarter, in_quarter)[...]

    def scatter_z(t):
        moved(1, t)
        kept[t][...] = sum(quarters[t][i] * matches(owner_x, i) for i in range(NX))

        @pl.loop(1, NZ)
        def _(k):
            to, device = along_z(k)
            move(2, t, of_half(kept[t], t, to * in_piece, in_piece), pieces[t].at[z], device).start()

        pieces[t][z] = of_half(kept[t], t, z * in_piece, in_piece)[...]

    def gather_z(t):
        moved(2, t)
        own_piece = of_full(full[t], t, core, x * in_quarter + z * in_piece, in_piece)
        own_piece[...] = sum(pieces[t][i] * matches(owner_z, i) for i in range(NZ))

        @pl.loop(1, NZ)
        def _(k):
            move(3, t, own_piece, own_piece, along_z(k)[1]).start()

    def gather_x(t):
        moved(3, t)
        own_quarter = of_full(full[t], t, core, x * in_quarter, in_quarter)
        for k in range(1, NX):
            move(4, t, own_quarter, own_quarter, along_x(k)[1]).start()

    def join_halves(t):
        moved(4, t)
        own_half = of_full(full[t], t, core, 0, in_half)
        move(5, t, own_half, own_half, twin).start()

    hot_at = pl.ds(0, HOT_ROWS)
    own_cols = pl.ds(pl.multiple_of(me * quarter, 128), quarter)
    top, group_tok = chosen.shape
    first_rows = (((0,), (0,)), ((), ()))

    def count(shape, axis):
        return lax.broadcasted_iota(jnp.int32, shape, axis)

    def as_ones(mask):
        return jnp.where(mask, 1.0, 0.0).astype(BF16)

    def turned(value):
        size = value.shape[0]
        eye = as_ones(count((size, size), 0) == count((size, size), 1))
        return lax.dot_general(value.astype(BF16), eye, first_rows, preferred_element_type=F32)

    high = mixing[...].astype(BF16)
    low = (mixing[...] - high.astype(F32)).astype(BF16)
    ids, high, low = chosen[...].astype(F32), high.astype(F32), low.astype(F32)
    expert = count((experts, group_tok), 0).astype(F32)
    member, weight_hi, weight_lo = (jnp.zeros((experts, group_tok), F32) for _ in range(3))
    for k in range(top):
        hit = ids[k : k + 1, :] == expert
        member += jnp.where(hit, 1.0, 0.0)
        weight_hi += jnp.where(hit, high[k : k + 1, :], 0.0)
        weight_lo += jnp.where(hit, low[k : k + 1, :], 0.0)
    earlier = as_ones(count((group_tok, group_tok), 0) < count((group_tok, group_tok), 1))
    rank = jnp.where(member > 0.0, dot(member.astype(BF16), earlier), -1.0)
    picks = jnp.sum(member, axis=1, keepdims=True)
    is_hot = picks == jnp.max(picks, axis=0, keepdims=True)
    cold_rank = jnp.where(is_hot, -1.0, rank)

    def of_hot(value):
        return jnp.sum(jnp.where(is_hot, value, 0.0), axis=0, keepdims=True)

    place = count((experts, 1), 0)
    z_bits = NZ.bit_length() - 1
    owner_core = of_hot((place & 1).astype(F32))
    owner_z = of_hot((lax.shift_right_logical(place, 1) & (NZ - 1)).astype(F32))
    owner_x = of_hot(lax.shift_right_logical(place, 1 + z_bits).astype(F32))

    def matches(value, index):
        return as_ones(value == jnp.asarray(index).astype(F32))

    hot_picked = of_hot(rank) == count((HOT_ROWS, group_tok), 0).astype(F32)
    hot_pick[...] = as_ones(hot_picked)
    hot_hi[...] = jnp.where(hot_picked, of_hot(weight_hi), 0.0).astype(BF16)
    hot_lo[...] = jnp.where(hot_picked, of_hot(weight_lo), 0.0).astype(BF16)

    def belongs(slot_at, expert_at):
        return as_ones(jnp.logical_and(slot_at >= expert_at * SLOT, slot_at < (expert_at + 1) * SLOT))

    @pl.loop(0, BLOCKS)
    def _(b):
        at = pl.ds(pl.multiple_of(b * padded, padded), padded)
        spread_out = belongs(count((padded, experts), 0) + b * padded, count((padded, experts), 1))
        slots = (count((padded, group_tok), 0) & (SLOT - 1)).astype(F32)
        pick = as_ones(dot(spread_out, cold_rank.astype(BF16)) == slots)
        sent[at, :] = dot(pick, tok[:, own_cols]).astype(BF16)

    def mixing_tables():
        by_token = [turned(value).astype(BF16) for value in (cold_rank, weight_hi, weight_lo)]

        @pl.loop(0, BLOCKS)
        def _(b):
            at = pl.ds(pl.multiple_of(b * padded, padded), padded)
            spread_out = belongs(count((experts, padded), 1) + b * padded, count((experts, padded), 0))
            slots = (count((group_tok, padded), 1) & (SLOT - 1)).astype(F32)
            picked = dot(by_token[0], spread_out) == slots
            mix_hi[:, at] = jnp.where(picked, dot(by_token[1], spread_out), 0.0).astype(BF16)
            mix_lo[:, at] = jnp.where(picked, dot(by_token[2], spread_out), 0.0).astype(BF16)

    pl.semaphore_wait(barrier, experts - 1 + n_dp - 1)

    def slot(i):
        return pl.ds(pl.multiple_of(i * SLOT, SLOT), SLOT)

    own = slot(mine)
    got[own, :] = sent[own, :]

    def exchange(src, dst, to, send_sem, recv_sem):
        return pltpu.make_async_remote_copy(
            src_ref=src.at[slot(to), :], dst_ref=dst.at[own, :], send_sem=send_sem, recv_sem=recv_sem,
            device_id={"expert": to}, device_id_type=MESH,
        )

    for j in range(BLOCKS):

        @pl.loop(1 if j == 0 else 0, per)
        def _(i, j=j):
            to = ((my_block + j) % BLOCKS) * per + (my_place + i) % per
            exchange(sent, got, to, disp_send, disp_recv.at[j]).start()

    for t in range(3):
        swap_halves(t)
    mixing_tables()

    def hot_units():
        acc_gate[hot_at, :] = jnp.zeros((HOT_ROWS, units), F32)
        acc_up[hot_at, :] = jnp.zeros((HOT_ROWS, units), F32)
        moved(5, 0)
        moved(5, 1)

        @pl.loop(0, n_dp)
        def _(q):
            cols = pl.ds(pl.multiple_of(q * quarter, quarter), quarter)
            inputs = dot(hot_pick[...], tok[:, cols]).astype(BF16)
            acc_gate[hot_at, :] += dot(inputs, hot_gate[cols, :])
            acc_up[hot_at, :] += dot(inputs, hot_up[cols, :])

        hot_rows[...] = (jax.nn.silu(acc_gate[hot_at, :]) * acc_up[hot_at, :]).astype(BF16)

    def hot_results():
        moved(5, 2)

        @pl.loop(0, n_dp)
        def _(q):
            cols = pl.ds(pl.multiple_of(q * quarter, quarter), quarter)
            hot_part[q, :, :] = dot(hot_rows[...], hot_down[:, cols]).astype(BF16)

        for k in range(1, n_dp):
            hot_copy(k).start()

    def hot_copy(k):
        to = (me + k) % n_dp
        return pltpu.make_async_remote_copy(
            src_ref=hot_part.at[to], dst_ref=hot_got.at[k - 1], send_sem=hot_send.at[k - 1],
            recv_sem=hot_recv.at[k - 1], device_id={"dp": to}, device_id_type=MESH,
        )

    def across_dp(kind, j, src, dst, to):
        return pltpu.make_async_remote_copy(
            src_ref=src, dst_ref=dst, send_sem=y_send.at[kind, j], recv_sem=y_recv.at[kind, j],
            device_id={"dp": to}, device_id_type=MESH,
        )

    def block_of(j):
        return (my_block + BLOCKS - j) % BLOCKS

    def packed_at(j):
        return pl.ds(pl.multiple_of(block_of(j) * packed, 16), packed)

    def padded_at(j):
        return pl.ds(pl.multiple_of(block_of(j) * padded, padded), padded)

    left, right = pl.ds(0, half), pl.ds(half, half)
    copies = {}

    def start(kind, j, src, dst, to):
        copies[kind, j] = across_dp(kind, j, src, dst, to)
        copies[kind, j].start()

    def gather_rows(j):
        take = per - 1 if j == 0 else per
        pltpu.make_async_copy(
            got.at[pl.ds(0, take * SLOT), :], got.at[pl.ds(0, take * SLOT), :], disp_recv.at[j]
        ).wait()
        at = packed_at(j)
        rows[me, at, :] = dot(pack[...], got[padded_at(j), :]).astype(BF16)
        start(0, j, rows.at[me, at, :], rows.at[me, at, :], above)
        start(1, j, rows.at[me, at, :], rows.at[me, at, :], below)

    def forward_rows(j):
        at = packed_at(j)
        copies[0, j].wait_recv()
        start(2, j, rows.at[below, at, left], rows.at[below, at, left], above)
        copies[1, j].wait_recv()
        start(3, j, rows.at[above, at, right], rows.at[above, at, right], below)

    def compute(j):
        at = packed_at(j)
        copies[2, j].wait_recv()
        copies[3, j].wait_recv()
        acc_gate[...] = jnp.zeros_like(acc_gate)
        acc_up[...] = jnp.zeros_like(acc_up)

        @pl.loop(0, n_dp)
        def _(q):
            depth = pl.ds(pl.multiple_of(q * quarter, quarter), quarter)
            acc_gate[...] += dot(rows[q, at, :], w_gate[depth, :])
            acc_up[...] += dot(rows[q, at, :], w_up[depth, :])

        hidden = (jax.nn.silu(acc_gate[...]) * acc_up[...]).astype(BF16)

        @pl.loop(0, n_dp)
        def _(i):
            q = (across + i) % n_dp
            cols = pl.ds(pl.multiple_of(q * quarter, quarter), quarter)
            part[q, at, :] = dot(hidden, w_down[:, cols]).astype(BF16)

        start(4, j, part.at[across, at, left], relay_up.at[at, :], above)
        start(5, j, part.at[across, at, right], relay_down.at[at, :], below)

    def relay(j):
        at = packed_at(j)
        copies[4, j].wait_recv()
        part[above, at, left] = (part[above, at, left].astype(F32) + relay_up[at, :].astype(F32)).astype(BF16)
        start(6, j, part.at[above, at, :], from_down.at[at, :], above)
        copies[5, j].wait_recv()
        part[below, at, right] = (part[below, at, right].astype(F32) + relay_down[at, :].astype(F32)).astype(BF16)
        start(7, j, part.at[below, at, :], from_up.at[at, :], below)

    def send_back(j):
        at, wide = packed_at(j), padded_at(j)
        copies[6, j].wait_recv()
        copies[7, j].wait_recv()
        total = part[me, at, :].astype(F32) + from_down[at, :].astype(F32) + from_up[at, :].astype(F32)
        spread[wide, :] = dot(unpack[...], total.astype(BF16)).astype(BF16)
        if j == 0:
            back[own, :] = spread[own, :]

        @pl.loop(1 if j == 0 else 0, per)
        def _(i):
            to = block_of(j) * per + (my_place + i) % per
            exchange(spread, back, to, back_send, back_recv).start()

    stages = (gather_rows, forward_rows, compute, relay, send_back)
    delays = (0, 1, 2, 3, 4)
    moves = (scatter_x, scatter_z, gather_z, gather_x, join_halves)
    turns = (0, 1, 2, 3, 5)
    for t in range(3):
        scatter_x(t)
    for step in range(max(BLOCKS + delays[-1], 2 + turns[-1])):
        for stage, delay in zip(stages, delays):
            if 0 <= step - delay < BLOCKS:
                stage(step - delay)
        for stage, turn in zip(moves[1:], turns[1:]):
            t = step + 1 - turn
            if 0 <= t < 3:
                stage(t)
    hot_units()
    hot_results()

    others = pl.ds(0, (experts - 1) * SLOT)
    pltpu.make_async_copy(back.at[others, :], back.at[others, :], back_recv).wait()
    mixed = dot(mix_hi[...], back[...]) + dot(mix_lo[...], back[...])
    hot_sum = hot_part[me, :, :].astype(F32)
    for k in range(1, n_dp):
        hot_copy(k).wait_recv()
        hot_sum += hot_got[k - 1, :, :].astype(F32)
    hot_sum = hot_sum.astype(BF16)
    mixed += lax.dot_general(hot_hi[...], hot_sum, first_rows, preferred_element_type=F32)
    mixed += lax.dot_general(hot_lo[...], hot_sum, first_rows, preferred_element_type=F32)
    out[...] = mixed.astype(BF16)

    pltpu.make_async_copy(sent.at[others, :], sent.at[others, :], disp_send).wait()
    pltpu.make_async_copy(spread.at[others, :], spread.at[others, :], back_send).wait()
    for copy in copies.values():
        copy.wait_send()
    for k in range(1, n_dp):
        hot_copy(k).wait_send()
    for t in range(3):
        for stage in range(6):
            moved(stage, t, move_send)


def local(tokens, routing, combine, *weights):
    tokens, routing, combine = tokens[0], routing[0].T, combine[0].T
    weights = [weight[0] for weight in weights]
    group_tok, width = tokens.shape
    experts, n_dp = lax.axis_size("expert"), lax.axis_size("dp")
    units, quarter, per = weights[0].shape[1], width // n_dp, experts // BLOCKS
    slots, held = experts * SLOT, experts * CAP
    block = per * CAP
    kept, kept_down = (width // (2 * NX), units), (units // 2, width // NX)
    piece, piece_down = (kept[0] // NZ, units), (units // 2, kept_down[1] // NZ)
    place = np.arange(block)
    wanted = (place // CAP) * SLOT + place % CAP
    pack = jnp.asarray(wanted[:, None] == np.arange(per * SLOT)[None, :], BF16)
    unpack = jnp.asarray(wanted[None, :] == np.arange(per * SLOT)[:, None], BF16)
    vmem, anywhere = pl.BlockSpec(memory_space=VMEM), pl.BlockSpec(memory_space=pl.ANY)
    dma = pltpu.SemaphoreType.DMA
    mixed = pl.pallas_call(
        experts_kernel,
        name="routed_experts",
        out_shape=jax.ShapeDtypeStruct((group_tok, quarter), BF16),
        in_specs=[vmem] * 5 + [anywhere] * 3,
        out_specs=vmem,
        scratch_shapes=[
            VMEM((group_tok, slots), BF16),
            VMEM((group_tok, slots), BF16),
            *[VMEM((HOT_ROWS, group_tok), BF16)] * 3,
            VMEM((slots, quarter), BF16),
            VMEM((slots, quarter), BF16),
            VMEM((n_dp, held, quarter), BF16),
            VMEM((n_dp, held, quarter), BF16),
            VMEM((held, quarter // 2), BF16),
            VMEM((held, quarter // 2), BF16),
            VMEM((held, quarter), BF16),
            VMEM((held, quarter), BF16),
            VMEM((slots, quarter), BF16),
            VMEM((slots, quarter), BF16),
            VMEM((width, units), BF16),
            VMEM((width, units), BF16),
            VMEM((units, width), BF16),
            VMEM((block, units), F32),
            VMEM((block, units), F32),
            VMEM((width, units), BF16),
            VMEM((width, units), BF16),
            VMEM((units, width), BF16),
            *[VMEM(shape, BF16) for shape in ((width // 2, units), (width // 2, units), (units // 2, width))],
            *[VMEM((NX, *shape), BF16) for shape in (kept, kept, kept_down)],
            *[VMEM(shape, BF16) for shape in (kept, kept, kept_down)],
            *[VMEM((NZ, *shape), BF16) for shape in (piece, piece, piece_down)],
            VMEM((HOT_ROWS, units), BF16),
            VMEM((n_dp, HOT_ROWS, quarter), BF16),
            VMEM((n_dp - 1, HOT_ROWS, quarter), BF16),
            dma((3,)),
            dma((6, 3)),
            dma((6, 3)),
            dma((n_dp - 1,)),
            dma((n_dp - 1,)),
            dma,
            dma((BLOCKS,)),
            dma((8, BLOCKS)),
            dma((8, BLOCKS)),
            dma,
            dma,
        ],
        compiler_params=pltpu.CompilerParams(vmem_limit_bytes=63 << 20, has_side_effects=True, collective_id=0),
        cost_estimate=pl.CostEstimate(
            flops=6 * held * width * units, bytes_accessed=60 << 20, transcendentals=held * units
        ),
    )(tokens, routing, combine, pack, unpack, *weights)
    return mixed[None]


def solution(mesh):
    placed = (
        P("expert", None, None),
        P("expert", None, None),
        P("expert", None, None),
        P("expert", None, "dp"),
        P("expert", None, "dp"),
        P("expert", "dp", None),
    )
    return jax.shard_map(
        local, mesh=mesh, in_specs=placed, out_specs=P("expert", None, "dp"), check_vma=False
    )
```

```python
import jax
import jax.numpy as jnp
import numpy as np
from jax import lax
from jax.experimental import pallas as pl
from jax.experimental.pallas import tpu as pltpu
from jax.sharding import PartitionSpec as P

CAP = 13
SLOT = 16
BLOCKS = 4
NX, NZ = 4, 8
HOT_ROWS = 48
MESH = pl.DeviceIdType.MESH
VMEM = pltpu.VMEM
BF16 = jnp.bfloat16
F32 = jnp.float32


def dot(a, b):
    return jnp.dot(a, b, preferred_element_type=F32)


def experts_kernel(
    tok, chosen, mixing, pack, unpack, gate_hbm, up_hbm, down_hbm, out,
    mix_hi, mix_lo, hot_pick, hot_hi, hot_lo,
    sent, got, rows, part, relay_up, relay_down, from_up, from_down, spread, back,
    w_gate, w_up, w_down, acc_gate, acc_up,
    hot_gate, hot_up, hot_down, half_gate, half_up, half_down, quarter_gate, quarter_up, quarter_down,
    kept_gate, kept_up, kept_down, piece_gate, piece_up, piece_down, hot_rows, hot_part, hot_got,
    load_sem, move_send, move_recv, hot_send, hot_recv, disp_send, disp_recv, y_send, y_recv, back_send, back_recv,
):
    n_dp, experts = rows.shape[0], got.shape[0] // SLOT
    per = experts // BLOCKS
    padded, packed = per * SLOT, per * CAP
    quarter = sent.shape[1]
    half = quarter // 2
    me, mine = lax.axis_index("dp"), lax.axis_index("expert")
    my_block, my_place = mine // per, mine % per
    above, below, across = (me + 1) % n_dp, (me + n_dp - 1) % n_dp, (me + 2) % n_dp

    barrier = pltpu.get_barrier_semaphore()

    @pl.loop(1, experts)
    def _(k):
        pl.semaphore_signal(barrier, inc=1, device_id={"expert": (mine + k) % experts}, device_id_type=MESH)

    for k in range(1, n_dp):
        pl.semaphore_signal(barrier, inc=1, device_id={"dp": (me + k) % n_dp}, device_id_type=MESH)

    x, z, core = mine // (2 * NZ), (mine // 2) % NZ, mine % 2
    given, held = (gate_hbm, up_hbm, down_hbm), (w_gate, w_up, w_down)
    loads = [pltpu.make_async_copy(src, dst, load_sem.at[i]) for i, (src, dst) in enumerate(zip(given, held))]
    for load in loads:
        load.start()

    full, halves = (hot_gate, hot_up, hot_down), (half_gate, half_up, half_down)
    quarters, kept = (quarter_gate, quarter_up, quarter_down), (kept_gate, kept_up, kept_down)
    pieces = (piece_gate, piece_up, piece_down)
    depth, units = w_gate.shape
    in_half, in_quarter, in_piece = depth // 2, depth // (2 * NX), depth // (2 * NX * NZ)

    def of_full(ref, t, lane, at, size):
        if t < 2:
            return ref.at[pl.ds(pl.multiple_of(lane * in_half + at, in_piece), size), :]
        rows_at = pl.ds(pl.multiple_of(lane * (units // 2), units // 2), units // 2)
        return ref.at[rows_at, pl.ds(pl.multiple_of(2 * at, 2 * in_piece), 2 * size)]

    def of_half(ref, t, at, size):
        if t < 2:
            return ref.at[pl.ds(pl.multiple_of(at, in_piece), size), :]
        return ref.at[:, pl.ds(pl.multiple_of(2 * at, 2 * in_piece), 2 * size)]

    def move(stage, t, src, dst, to):
        return pltpu.make_async_remote_copy(
            src_ref=src, dst_ref=dst, send_sem=move_send.at[stage, t], recv_sem=move_recv.at[stage, t],
            device_id={"expert": to}, device_id_type=MESH,
        )

    def moved_amount(stage, t):
        if stage in (0, 5):
            return halves[t]
        return quarters[t].at[pl.ds(0, NX - 1)] if stage in (1, 4) else pieces[t].at[pl.ds(0, NZ - 1)]

    def moved(stage, t, sems=move_recv):
        amount = moved_amount(stage, t)
        pltpu.make_async_copy(amount, amount, sems.at[stage, t]).wait()

    twin = mine + 1 - 2 * core

    def along_x(k):
        to = (x + k) % NX
        return to, (to * NZ + z) * 2 + core

    def along_z(k):
        to = (z + k) % NZ
        return to, (x * NZ + to) * 2 + core

    def swap_halves(t):
        move(0, t, of_full(given[t], t, 1 - core, 0, in_half), halves[t], twin).start()

    def scatter_x(t):
        loads[t].wait()
        moved(0, t)

        @pl.loop(0, 8)
        def _(i):
            here = of_half(halves[t], t, i * (in_half // 8), in_half // 8)
            ours = of_full(held[t], t, core, i * (in_half // 8), in_half // 8)
            here[...] = ours[...] * matches(owner_core, core) + here[...] * matches(owner_core, 1 - core)

        for k in range(1, NX):
            to, device = along_x(k)
            move(1, t, of_half(halves[t], t, to * in_quarter, in_quarter), quarters[t].at[x], device).start()
        quarters[t][x] = of_half(halves[t], t, x * in_quarter, in_quarter)[...]

    def scatter_z(t):
        moved(1, t)
        kept[t][...] = sum(quarters[t][i] * matches(owner_x, i) for i in range(NX))

        @pl.loop(1, NZ)
        def _(k):
            to, device = along_z(k)
            move(2, t, of_half(kept[t], t, to * in_piece, in_piece), pieces[t].at[z], device).start()

        pieces[t][z] = of_half(kept[t], t, z * in_piece, in_piece)[...]

    def gather_z(t):
        moved(2, t)
        own_piece = of_full(full[t], t, core, x * in_quarter + z * in_piece, in_piece)
        own_piece[...] = sum(pieces[t][i] * matches(owner_z, i) for i in range(NZ))

        @pl.loop(1, NZ)
        def _(k):
            move(3, t, own_piece, own_piece, along_z(k)[1]).start()

    def gather_x(t):
        moved(3, t)
        own_quarter = of_full(full[t], t, core, x * in_quarter, in_quarter)
        for k in range(1, NX):
            move(4, t, own_quarter, own_quarter, along_x(k)[1]).start()

    def join_halves(t):
        moved(4, t)
        own_half = of_full(full[t], t, core, 0, in_half)
        move(5, t, own_half, own_half, twin).start()

    hot_at = pl.ds(0, HOT_ROWS)
    own_cols = pl.ds(pl.multiple_of(me * quarter, 128), quarter)
    top, group_tok = chosen.shape
    first_rows = (((0,), (0,)), ((), ()))

    def count(shape, axis):
        return lax.broadcasted_iota(jnp.int32, shape, axis)

    def as_ones(mask):
        return jnp.where(mask, 1.0, 0.0).astype(BF16)

    def turned(value):
        size = value.shape[0]
        eye = as_ones(count((size, size), 0) == count((size, size), 1))
        return lax.dot_general(value.astype(BF16), eye, first_rows, preferred_element_type=F32)

    high = mixing[...].astype(BF16)
    low = (mixing[...] - high.astype(F32)).astype(BF16)
    ids, high, low = chosen[...].astype(F32), high.astype(F32), low.astype(F32)
    expert = count((experts, group_tok), 0).astype(F32)
    member, weight_hi, weight_lo = (jnp.zeros((experts, group_tok), F32) for _ in range(3))
    for k in range(top):
        hit = ids[k : k + 1, :] == expert
        member += jnp.where(hit, 1.0, 0.0)
        weight_hi += jnp.where(hit, high[k : k + 1, :], 0.0)
        weight_lo += jnp.where(hit, low[k : k + 1, :], 0.0)
    earlier = as_ones(count((group_tok, group_tok), 0) < count((group_tok, group_tok), 1))
    rank = jnp.where(member > 0.0, dot(member.astype(BF16), earlier), -1.0)
    picks = jnp.sum(member, axis=1, keepdims=True)
    is_hot = picks == jnp.max(picks, axis=0, keepdims=True)
    cold_rank = jnp.where(is_hot, -1.0, rank)

    def of_hot(value):
        return jnp.sum(jnp.where(is_hot, value, 0.0), axis=0, keepdims=True)

    place = count((experts, 1), 0)
    z_bits = NZ.bit_length() - 1
    owner_core = of_hot((place & 1).astype(F32))
    owner_z = of_hot((lax.shift_right_logical(place, 1) & (NZ - 1)).astype(F32))
    owner_x = of_hot(lax.shift_right_logical(place, 1 + z_bits).astype(F32))

    def matches(value, index):
        return as_ones(value == jnp.asarray(index).astype(F32))

    hot_picked = of_hot(rank) == count((HOT_ROWS, group_tok), 0).astype(F32)
    hot_pick[...] = as_ones(hot_picked)
    hot_hi[...] = jnp.where(hot_picked, of_hot(weight_hi), 0.0).astype(BF16)
    hot_lo[...] = jnp.where(hot_picked, of_hot(weight_lo), 0.0).astype(BF16)

    def belongs(slot_at, expert_at):
        return as_ones(jnp.logical_and(slot_at >= expert_at * SLOT, slot_at < (expert_at + 1) * SLOT))

    @pl.loop(0, BLOCKS)
    def _(b):
        at = pl.ds(pl.multiple_of(b * padded, padded), padded)
        spread_out = belongs(count((padded, experts), 0) + b * padded, count((padded, experts), 1))
        slots = (count((padded, group_tok), 0) & (SLOT - 1)).astype(F32)
        pick = as_ones(dot(spread_out, cold_rank.astype(BF16)) == slots)
        sent[at, :] = dot(pick, tok[:, own_cols]).astype(BF16)

    def mixing_tables():
        by_token = [turned(value).astype(BF16) for value in (cold_rank, weight_hi, weight_lo)]

        @pl.loop(0, BLOCKS)
        def _(b):
            at = pl.ds(pl.multiple_of(b * padded, padded), padded)
            spread_out = belongs(count((experts, padded), 1) + b * padded, count((experts, padded), 0))
            slots = (count((group_tok, padded), 1) & (SLOT - 1)).astype(F32)
            picked = dot(by_token[0], spread_out) == slots
            mix_hi[:, at] = jnp.where(picked, dot(by_token[1], spread_out), 0.0).astype(BF16)
            mix_lo[:, at] = jnp.where(picked, dot(by_token[2], spread_out), 0.0).astype(BF16)

    pl.semaphore_wait(barrier, experts - 1 + n_dp - 1)

    def slot(i):
        return pl.ds(pl.multiple_of(i * SLOT, SLOT), SLOT)

    own = slot(mine)
    got[own, :] = sent[own, :]

    def exchange(src, dst, to, send_sem, recv_sem):
        return pltpu.make_async_remote_copy(
            src_ref=src.at[slot(to), :], dst_ref=dst.at[own, :], send_sem=send_sem, recv_sem=recv_sem,
            device_id={"expert": to}, device_id_type=MESH,
        )

    for t in range(3):
        swap_halves(t)

    for j in range(BLOCKS):

        @pl.loop(1 if j == 0 else 0, per)
        def _(i, j=j):
            to = ((my_block + j) % BLOCKS) * per + (my_place + i) % per
            exchange(sent, got, to, disp_send, disp_recv.at[j]).start()

    mixing_tables()

    def hot_units():
        acc_gate[hot_at, :] = jnp.zeros((HOT_ROWS, units), F32)
        acc_up[hot_at, :] = jnp.zeros((HOT_ROWS, units), F32)
        moved(5, 0)
        moved(5, 1)

        @pl.loop(0, n_dp)
        def _(q):
            cols = pl.ds(pl.multiple_of(q * quarter, quarter), quarter)
            inputs = dot(hot_pick[...], tok[:, cols]).astype(BF16)
            acc_gate[hot_at, :] += dot(inputs, hot_gate[cols, :])
            acc_up[hot_at, :] += dot(inputs, hot_up[cols, :])

        hot_rows[...] = (jax.nn.silu(acc_gate[hot_at, :]) * acc_up[hot_at, :]).astype(BF16)

    def hot_results():
        moved(5, 2)

        @pl.loop(0, n_dp)
        def _(q):
            cols = pl.ds(pl.multiple_of(q * quarter, quarter), quarter)
            hot_part[q, :, :] = dot(hot_rows[...], hot_down[:, cols]).astype(BF16)

        for k in range(1, n_dp):
            hot_copy(k).start()

    def hot_copy(k):
        to = (me + k) % n_dp
        return pltpu.make_async_remote_copy(
            src_ref=hot_part.at[to], dst_ref=hot_got.at[k - 1], send_sem=hot_send.at[k - 1],
            recv_sem=hot_recv.at[k - 1], device_id={"dp": to}, device_id_type=MESH,
        )

    def across_dp(kind, j, src, dst, to):
        return pltpu.make_async_remote_copy(
            src_ref=src, dst_ref=dst, send_sem=y_send.at[kind, j], recv_sem=y_recv.at[kind, j],
            device_id={"dp": to}, device_id_type=MESH,
        )

    def block_of(j):
        return (my_block + BLOCKS - j) % BLOCKS

    def packed_at(j):
        return pl.ds(pl.multiple_of(block_of(j) * packed, 16), packed)

    def padded_at(j):
        return pl.ds(pl.multiple_of(block_of(j) * padded, padded), padded)

    left, right = pl.ds(0, half), pl.ds(half, half)
    copies = {}

    def start(kind, j, src, dst, to):
        copies[kind, j] = across_dp(kind, j, src, dst, to)
        copies[kind, j].start()

    def gather_rows(j):
        take = per - 1 if j == 0 else per
        pltpu.make_async_copy(
            got.at[pl.ds(0, take * SLOT), :], got.at[pl.ds(0, take * SLOT), :], disp_recv.at[j]
        ).wait()
        at = packed_at(j)
        rows[me, at, :] = dot(pack[...], got[padded_at(j), :]).astype(BF16)
        start(0, j, rows.at[me, at, :], rows.at[me, at, :], above)
        start(1, j, rows.at[me, at, :], rows.at[me, at, :], below)

    def forward_rows(j):
        at = packed_at(j)
        copies[0, j].wait_recv()
        start(2, j, rows.at[below, at, left], rows.at[below, at, left], above)
        copies[1, j].wait_recv()
        start(3, j, rows.at[above, at, right], rows.at[above, at, right], below)

    def compute(j):
        at = packed_at(j)
        copies[2, j].wait_recv()
        copies[3, j].wait_recv()
        acc_gate[...] = jnp.zeros_like(acc_gate)
        acc_up[...] = jnp.zeros_like(acc_up)

        @pl.loop(0, n_dp)
        def _(q):
            depth = pl.ds(pl.multiple_of(q * quarter, quarter), quarter)
            acc_gate[...] += dot(rows[q, at, :], w_gate[depth, :])
            acc_up[...] += dot(rows[q, at, :], w_up[depth, :])

        hidden = (jax.nn.silu(acc_gate[...]) * acc_up[...]).astype(BF16)

        @pl.loop(0, n_dp)
        def _(i):
            q = (across + i) % n_dp
            cols = pl.ds(pl.multiple_of(q * quarter, quarter), quarter)
            part[q, at, :] = dot(hidden, w_down[:, cols]).astype(BF16)

        start(4, j, part.at[across, at, left], relay_up.at[at, :], above)
        start(5, j, part.at[across, at, right], relay_down.at[at, :], below)

    def relay(j):
        at = packed_at(j)
        copies[4, j].wait_recv()
        part[above, at, left] = (part[above, at, left].astype(F32) + relay_up[at, :].astype(F32)).astype(BF16)
        start(6, j, part.at[above, at, :], from_down.at[at, :], above)
        copies[5, j].wait_recv()
        part[below, at, right] = (part[below, at, right].astype(F32) + relay_down[at, :].astype(F32)).astype(BF16)
        start(7, j, part.at[below, at, :], from_up.at[at, :], below)

    def send_back(j):
        at, wide = packed_at(j), padded_at(j)
        copies[6, j].wait_recv()
        copies[7, j].wait_recv()
        total = part[me, at, :].astype(F32) + from_down[at, :].astype(F32) + from_up[at, :].astype(F32)
        spread[wide, :] = dot(unpack[...], total.astype(BF16)).astype(BF16)
        if j == 0:
            back[own, :] = spread[own, :]

        @pl.loop(1 if j == 0 else 0, per)
        def _(i):
            to = block_of(j) * per + (my_place + i) % per
            exchange(spread, back, to, back_send, back_recv).start()

    stages = (gather_rows, forward_rows, compute, relay, send_back)
    delays = (0, 1, 2, 3, 4)
    moves = (scatter_x, scatter_z, gather_z, gather_x, join_halves)
    turns = (0, 1, 2, 3, 5)
    scatter_x(0)
    for step in range(max(BLOCKS + delays[-1], 2 + turns[-1])):
        for stage, delay in zip(stages, delays):
            if 0 <= step - delay < BLOCKS:
                stage(step - delay)
        for stage, turn in zip(moves, turns):
            t = step + 1 - turn
            if 0 <= t < 3:
                stage(t)
    hot_units()
    hot_results()

    others = pl.ds(0, (experts - 1) * SLOT)
    pltpu.make_async_copy(back.at[others, :], back.at[others, :], back_recv).wait()
    mixed = dot(mix_hi[...], back[...]) + dot(mix_lo[...], back[...])
    hot_sum = hot_part[me, :, :].astype(F32)
    for k in range(1, n_dp):
        hot_copy(k).wait_recv()
        hot_sum += hot_got[k - 1, :, :].astype(F32)
    hot_sum = hot_sum.astype(BF16)
    mixed += lax.dot_general(hot_hi[...], hot_sum, first_rows, preferred_element_type=F32)
    mixed += lax.dot_general(hot_lo[...], hot_sum, first_rows, preferred_element_type=F32)
    out[...] = mixed.astype(BF16)

    pltpu.make_async_copy(sent.at[others, :], sent.at[others, :], disp_send).wait()
    pltpu.make_async_copy(spread.at[others, :], spread.at[others, :], back_send).wait()
    for copy in copies.values():
        copy.wait_send()
    for k in range(1, n_dp):
        hot_copy(k).wait_send()
    for t in range(3):
        for stage in range(6):
            moved(stage, t, move_send)


def local(tokens, routing, combine, *weights):
    tokens, routing, combine = tokens[0], routing[0].T, combine[0].T
    weights = [weight[0] for weight in weights]
    group_tok, width = tokens.shape
    experts, n_dp = lax.axis_size("expert"), lax.axis_size("dp")
    units, quarter, per = weights[0].shape[1], width // n_dp, experts // BLOCKS
    slots, held = experts * SLOT, experts * CAP
    block = per * CAP
    kept, kept_down = (width // (2 * NX), units), (units // 2, width // NX)
    piece, piece_down = (kept[0] // NZ, units), (units // 2, kept_down[1] // NZ)
    place = np.arange(block)
    wanted = (place // CAP) * SLOT + place % CAP
    pack = jnp.asarray(wanted[:, None] == np.arange(per * SLOT)[None, :], BF16)
    unpack = jnp.asarray(wanted[None, :] == np.arange(per * SLOT)[:, None], BF16)
    vmem, anywhere = pl.BlockSpec(memory_space=VMEM), pl.BlockSpec(memory_space=pl.ANY)
    dma = pltpu.SemaphoreType.DMA
    mixed = pl.pallas_call(
        experts_kernel,
        name="routed_experts",
        out_shape=jax.ShapeDtypeStruct((group_tok, quarter), BF16),
        in_specs=[vmem] * 5 + [anywhere] * 3,
        out_specs=vmem,
        scratch_shapes=[
            VMEM((group_tok, slots), BF16),
            VMEM((group_tok, slots), BF16),
            *[VMEM((HOT_ROWS, group_tok), BF16)] * 3,
            VMEM((slots, quarter), BF16),
            VMEM((slots, quarter), BF16),
            VMEM((n_dp, held, quarter), BF16),
            VMEM((n_dp, held, quarter), BF16),
            VMEM((held, quarter // 2), BF16),
            VMEM((held, quarter // 2), BF16),
            VMEM((held, quarter), BF16),
            VMEM((held, quarter), BF16),
            VMEM((slots, quarter), BF16),
            VMEM((slots, quarter), BF16),
            VMEM((width, units), BF16),
            VMEM((width, units), BF16),
            VMEM((units, width), BF16),
            VMEM((block, units), F32),
            VMEM((block, units), F32),
            VMEM((width, units), BF16),
            VMEM((width, units), BF16),
            VMEM((units, width), BF16),
            *[VMEM(shape, BF16) for shape in ((width // 2, units), (width // 2, units), (units // 2, width))],
            *[VMEM((NX, *shape), BF16) for shape in (kept, kept, kept_down)],
            *[VMEM(shape, BF16) for shape in (kept, kept, kept_down)],
            *[VMEM((NZ, *shape), BF16) for shape in (piece, piece, piece_down)],
            VMEM((HOT_ROWS, units), BF16),
            VMEM((n_dp, HOT_ROWS, quarter), BF16),
            VMEM((n_dp - 1, HOT_ROWS, quarter), BF16),
            dma((3,)),
            dma((6, 3)),
            dma((6, 3)),
            dma((n_dp - 1,)),
            dma((n_dp - 1,)),
            dma,
            dma((BLOCKS,)),
            dma((8, BLOCKS)),
            dma((8, BLOCKS)),
            dma,
            dma,
        ],
        compiler_params=pltpu.CompilerParams(vmem_limit_bytes=63 << 20, has_side_effects=True, collective_id=0),
        cost_estimate=pl.CostEstimate(
            flops=6 * held * width * units, bytes_accessed=60 << 20, transcendentals=held * units
        ),
    )(tokens, routing, combine, pack, unpack, *weights)
    return mixed[None]


def solution(mesh):
    placed = (
        P("expert", None, None),
        P("expert", None, None),
        P("expert", None, None),
        P("expert", None, "dp"),
        P("expert", None, "dp"),
        P("expert", "dp", None),
    )
    return jax.shard_map(
        local, mesh=mesh, in_specs=placed, out_specs=P("expert", None, "dp"), check_vma=False
    )
```
